32 devices in a mesh: row: 8 (over z, y), col: 4 (over x, core).
Axes of the slice: x: 2, y: 2, z: 4, core: 2. Of those that a mesh axis runs over, the one named last changes fastest.
Arguments:
- state: float32 [2, 8192, 8192], P(None, 'row', 'col'), as said below
- tile_vals: float32 [64, 2, 128, 128], P(('row', 'col')), may hold values from -0.375 to 0.375
- tile_row: int32 [64], P(('row', 'col')), may hold values from 0 to 63, as said below
- tile_col: int32 [64], P(('row', 'col')), may hold values from 0 to 63, as said below
- tile_op: int32 [64], P(('row', 'col')), may hold values from 0 to 16, as said below
Outputs:
- evolved: float32 [2, 8192, 8192], P(None, 'row', 'col')
The draws below stay inside these ranges and needn't reach their ends.
Inputs may be any that keep to these rules, and one draw needn't show every extreme that they name: Hermitian: state[0] is symmetric and state[1] antisymmetric. `tile_row`: in each aligned block of 8 entries (the tiles stored on the devices of one index of row), at most 2 lie in any one row slab, the tile rows 8 * s to 8 * s + 7 for s < 8. tile_col equals tile_row or tile_row + 1. `tile_op`: value 16 marks the effective Hamiltonian, smaller values the jump operators. Among the tiles whose rows lie in one row slab, at most 2 carry any one value.
All inputs are finite; a program needn't handle non-finite values.
Results may differ from the reference program's by a relative error of at most 0.0001.
Values sent between devices are 32-bit elements; how exact they have to be, the bound alone decides.
No kernel may reach another device: no remote copies, remote signals or barrier semaphores. Data moves between devices by JAX's collectives and lax.ppermute only.
A program may use at most 256 MiB of HBM per device.

```python
import jax
import jax.numpy as jnp
import numpy as np
from jax import lax

NDIM = 8192
NOPS = 16
TILE = 128
CAP = 2
TGRID = 64
SLABS = 8
TILES = 64


def tile_pattern(key):
    group_total = SLABS
    row_span = TGRID // SLABS
    key_list = jax.random.split(jax.random.fold_in(key, 71), 5)
    busy_slab = jax.random.randint(key_list[0], (), 0, group_total, dtype=jnp.int32)
    pair_total = (group_total - 2) // 4
    single_total = group_total - 2 - 2 * pair_total
    pick_table = np.array([entry // 2 for entry in range(2 * pair_total)] + [pair_total + entry for entry in range(single_total)], dtype=np.int32)

    def one_group(group_key):
        split_keys = jax.random.split(group_key, 2)
        shuffled = jax.random.permutation(split_keys[0], group_total - 1).astype(jnp.int32)
        others = shuffled + (shuffled >= busy_slab).astype(jnp.int32)
        labels = jnp.concatenate([jnp.stack([busy_slab, busy_slab]), others[pick_table]])
        return jax.random.permutation(split_keys[1], labels)
    slabs_all = jax.vmap(one_group)(jax.random.split(key_list[1], group_total))
    slab_flat = slabs_all.reshape(-1).astype(jnp.int32)
    group_ids = jnp.repeat(jnp.arange(group_total, dtype=jnp.int32), group_total)
    tile_rows = slab_flat * row_span + jax.random.randint(key_list[2], slab_flat.shape, 0, row_span, dtype=jnp.int32)
    tile_cols = jnp.minimum(tile_rows + jax.random.randint(key_list[3], slab_flat.shape, 0, 2, dtype=jnp.int32), TGRID - 1)

    def one_order(order_key):
        return jax.random.permutation(order_key, NOPS + 1).astype(jnp.int32)
    op_table = jax.vmap(one_order)(jax.random.split(key_list[4], group_total))
    tile_ops = op_table[slab_flat, group_ids]
    return (tile_rows, tile_cols, tile_ops)


def draw_tile_row(key, part):
    return tile_pattern(key)[0]


def draw_tile_col(key, part):
    return tile_pattern(key)[1]


def draw_tile_op(key, part):
    return tile_pattern(key)[2]


def draw_state(key, part):
    key_list = jax.random.split(jax.random.fold_in(key, 29), 2)
    first = jax.random.normal(key_list[0], (NDIM, NDIM), jnp.float32)
    second = jax.random.normal(key_list[1], (NDIM, NDIM), jnp.float32)
    real_part = 0.5 * (first + first.T)
    imag_part = 0.5 * (second - second.T)
    return jnp.stack([real_part, imag_part])


def block_levels(stream_key, shape, pieces, smallest, high):
    level, own = 1.0, jax.random.fold_in(stream_key, 6)
    for dim, blocks in pieces:
        steps = jnp.exp(jax.random.uniform(jax.random.fold_in(own, dim), (blocks,), jnp.float32, smallest / len(pieces), high / len(pieces)))
        level = level * jnp.repeat(steps, shape[dim] // blocks).reshape([-1 if axis == dim else 1 for axis in range(len(shape))])
    return level


def normal_values(rng, shape, width, most, cuts=(), kind=jnp.bfloat16):
    loudness = block_levels(rng, shape, cuts, -0.22, 0.18) if cuts else 1.0
    values = jax.random.normal(rng, shape, jnp.float32) * width * loudness
    return jnp.minimum(jnp.maximum(values, -most), most).astype(kind)


def setup_inputs(seed: int = 0) -> dict:
    keys = jax.random.split(jax.random.key(seed), 6)
    return {
        "state": draw_state(jax.random.fold_in(keys[5], 71), 0),
        "tile_vals": normal_values(keys[1], (TILES, 2, TILE, TILE), (2 * TILE) ** -0.5, 0.375, ((0, 32),), jnp.float32),
        "tile_row": draw_tile_row(jax.random.fold_in(keys[5], 71), 0),
        "tile_col": draw_tile_col(jax.random.fold_in(keys[5], 71), 0),
        "tile_op": draw_tile_op(jax.random.fold_in(keys[5], 71), 0),
    }


PRECISE = lax.Precision.HIGHEST
TIME_STEP = 0.25


def complex_product(formula, left_part, right_part):
    real_prod = jnp.einsum(formula, left_part[0], right_part[0], precision=PRECISE, preferred_element_type=jnp.float32)
    imag_prod = jnp.einsum(formula, left_part[1], right_part[1], precision=PRECISE, preferred_element_type=jnp.float32)
    mixed_prod = jnp.einsum(formula, left_part[0] + left_part[1], right_part[0] + right_part[1], precision=PRECISE, preferred_element_type=jnp.float32)
    return jnp.stack([real_prod - imag_prod, mixed_prod - real_prod - imag_prod])


def adjoint(tile_set):
    return jnp.stack([jnp.swapaxes(tile_set[0], -1, -2), -jnp.swapaxes(tile_set[1], -1, -2)])


def times_minus_i(values):
    return jnp.stack([values[1], -values[0]])


def times_i(values):
    return jnp.stack([-values[1], values[0]])


def compact(tile_set, row_ids, col_ids, op_ids, capacity, kind_count):
    slot_total = op_ids.shape[0]
    position = jnp.arange(slot_total, dtype=jnp.int32)
    earlier = (op_ids[:, None] == op_ids[None, :]) & (position[None, :] < position[:, None])
    rank_ids = jnp.sum(earlier.astype(jnp.int32), axis=1, dtype=jnp.int32)
    size_all = kind_count * capacity
    target = jnp.where(op_ids >= 0, op_ids * capacity + rank_ids, size_all).astype(jnp.int32)
    packed = jnp.zeros((size_all,) + tile_set.shape[1:], jnp.float32).at[target].set(tile_set, mode="drop")
    packed_rows = jnp.zeros((size_all,), jnp.int32).at[target].set(row_ids, mode="drop")
    packed_cols = jnp.zeros((size_all,), jnp.int32).at[target].set(col_ids, mode="drop")
    return (packed.reshape((kind_count, capacity) + tile_set.shape[1:]),
            packed_rows.reshape(kind_count, capacity),
            packed_cols.reshape(kind_count, capacity))


def rate_of(current, packed_tiles, packed_rows, packed_cols):
    grid = NDIM // TILE
    width_all = packed_rows.shape[1]
    extended = jnp.pad(current, ((0, 0), (0, TILE), (0, TILE)))
    row_strips = extended.reshape(2, grid + 1, TILE, NDIM + TILE)
    rate_sum = jnp.zeros_like(current)
    ham_tiles = jnp.moveaxis(packed_tiles[NOPS], 1, 0)
    ham_strips = row_strips[:, packed_cols[NOPS], :, :NDIM]
    ham_left = times_minus_i(complex_product("wij,wjn->win", ham_tiles, ham_strips))
    rate_sum = rate_sum.reshape(2, grid, TILE, NDIM).at[:, packed_rows[NOPS]].add(ham_left).reshape(current.shape)
    col_strips = extended[:, :NDIM, :].reshape(2, NDIM, grid + 1, TILE)
    ham_cols = col_strips[:, :, packed_cols[NOPS], :]
    ham_right = times_i(complex_product("nwj,wjk->nwk", ham_cols, adjoint(ham_tiles)))
    rate_sum = rate_sum.reshape(2, NDIM, grid, TILE).at[:, :, packed_rows[NOPS]].add(ham_right).reshape(current.shape)

    def one_jump(running, packed):
        jump_tiles, jump_rows, jump_cols = packed
        comp_tiles = jnp.moveaxis(jump_tiles, 1, 0)
        strips = row_strips[:, jump_cols]
        product = complex_product("aij,ajn->ain", comp_tiles, strips)
        panels = product.reshape(2, width_all, TILE, grid + 1, TILE)[:, :, :, jump_cols, :]
        contrib = complex_product("aibj,bjk->aibk", panels, adjoint(comp_tiles))
        placed = jnp.transpose(contrib, (1, 3, 0, 2, 4))
        grid_view = running.reshape(2, grid, TILE, grid, TILE)
        grid_view = grid_view.at[:, jump_rows[:, None], :, jump_rows[None, :], :].add(placed)
        return grid_view.reshape(current.shape), None

    rate_sum, unused = lax.scan(one_jump, rate_sum, (packed_tiles[:NOPS], packed_rows[:NOPS], packed_cols[:NOPS]))
    return rate_sum


def reference(state, tile_vals, tile_row, tile_col, tile_op):
    packed_tiles, packed_rows, packed_cols = compact(tile_vals, tile_row, tile_col, tile_op, SLABS * CAP, NOPS + 1)
    first_rate = rate_of(state, packed_tiles, packed_rows, packed_cols)
    middle = state + (0.5 * TIME_STEP) * first_rate
    second_rate = rate_of(middle, packed_tiles, packed_rows, packed_cols)
    return state + TIME_STEP * second_rate
```

```python
import functools

import jax
import jax.numpy as jnp
from jax import lax
from jax.experimental import pallas as pl
from jax.experimental.pallas import tpu as pltpu
from jax.sharding import PartitionSpec as P

NOPS = 16
CAP = 2
TIME_STEP = 0.25
UNROLL = 4
RING = 8
BOTH = ("row", "col")
ANY = pl.BlockSpec(memory_space=pl.ANY)
SMEM = pl.BlockSpec(memory_space=pltpu.SMEM)


class Sizes:
    def __init__(self, state, tile_vals):
        self.row_total = lax.axis_size("row")
        self.col_total = lax.axis_size("col")
        self.edge = tile_vals.shape[-1]
        self.own = tile_vals.shape[0]
        self.total = self.own * self.row_total * self.col_total
        self.rt = state.shape[1] // self.edge
        self.ct = state.shape[2] // self.edge
        self.span = self.ct // self.rt
        self.left_max = CAP * self.row_total
        self.right_max = self.span * self.left_max
        self.right_op = self.span * CAP
        self.pair_max = self.left_max * self.right_op
        self.pair_pad = -(-self.pair_max // UNROLL) * UNROLL
        self.wide = self.ct + 1
        place = 0
        for name, length in (
            ("counts", 8),
            ("left_tile", self.left_max),
            ("right_tile", self.right_max),
            ("kl_tile", CAP),
            ("kl_dst", CAP),
            ("kl_src", CAP),
            ("kr_tile", self.right_op),
            ("kr_dst", self.right_op),
            ("kr_src", self.right_op),
            ("pair_left", self.pair_pad),
            ("pair_right", self.pair_pad),
            ("pair_src", self.pair_pad),
            ("pair_dst", self.pair_pad),
            ("need", (self.rt + 1) * self.wide),
            ("touch", self.rt * self.ct),
            ("send_row", self.ct),
            ("send_col", self.rt),
            ("send_corner", 1),
        ):
            setattr(self, "at_" + name, place)
            place += length
        self.plan_size = -(-place // 128) * 128


N_LEFT, N_RIGHT, N_KL, N_KR, N_PAIR = range(5)


def plan_kernel(z, here, meta, plan, rlist, llist, slot):
    me_row, me_col = here[0], here[1]
    rt, ct, wide = z.rt, z.ct, z.wide

    def row_of(t):
        return meta[t]

    def col_of(t):
        return meta[z.total + t]

    def op_of(t):
        return meta[2 * z.total + t]

    @pl.loop(0, z.plan_size)
    def _(k):
        plan[k] = 0

    @pl.loop(0, z.pair_pad)
    def _(k):
        plan[z.at_pair_dst + k] = rt * ct

    row_base = me_row * rt
    col_base = me_col * ct

    def gather(t, found):
        n_left, n_right = found
        r = row_of(t)
        is_left = (r >= row_base) & (r < row_base + rt)
        is_right = (r >= col_base) & (r < col_base + ct)

        @pl.when(is_left)
        def _():
            llist[n_left] = t

        @pl.when(is_right)
        def _():
            rlist[n_right] = t
            slot[n_right] = -1

        return (
            n_left + is_left.astype(jnp.int32),
            n_right + is_right.astype(jnp.int32),
        )

    n_left, n_right = lax.fori_loop(0, z.total, gather, (jnp.int32(0), jnp.int32(0)))

    def one_left(a, _):
        t = llist[a]
        op = op_of(t)
        r1 = row_of(t) - row_base
        c1 = col_of(t) - row_base

        @pl.when(op == NOPS)
        def _():
            k = plan[z.at_counts + N_KL]
            plan[z.at_kl_tile + k] = t
            plan[z.at_kl_dst + k] = r1 * ct
            plan[z.at_kl_src + k] = c1 * wide
            plan[z.at_counts + N_KL] = k + 1

            @pl.loop(0, ct)
            def _(c):
                plan[z.at_need + c1 * wide + c] = 1
                plan[z.at_touch + r1 * ct + c] = 1

        @pl.when(op != NOPS)
        def _():
            first = plan[z.at_counts + N_PAIR]
            mine = plan[z.at_counts + N_LEFT]

            def one_right(b, _):
                u = rlist[b]

                @pl.when(op_of(u) == op)
                def _():
                    @pl.when(slot[b] < 0)
                    def _():
                        s = plan[z.at_counts + N_RIGHT]
                        slot[b] = s
                        plan[z.at_right_tile + s] = u
                        plan[z.at_counts + N_RIGHT] = s + 1

                    k = plan[z.at_counts + N_PAIR]
                    r2 = row_of(u) - col_base
                    c2 = col_of(u) - col_base
                    plan[z.at_pair_left + k] = mine
                    plan[z.at_pair_right + k] = slot[b]
                    plan[z.at_pair_src + k] = c1 * wide + c2
                    plan[z.at_pair_dst + k] = r1 * ct + r2
                    plan[z.at_need + c1 * wide + c2] = 1
                    plan[z.at_touch + r1 * ct + r2] = 1
                    plan[z.at_counts + N_PAIR] = k + 1

                return 0

            lax.fori_loop(0, n_right, one_right, 0)

            @pl.when(plan[z.at_counts + N_PAIR] > first)
            def _():
                plan[z.at_left_tile + mine] = t
                plan[z.at_counts + N_LEFT] = mine + 1

        return 0

    lax.fori_loop(0, n_left, one_left, 0)

    def one_kr(b, _):
        u = rlist[b]

        @pl.when(op_of(u) == NOPS)
        def _():
            k = plan[z.at_counts + N_KR]
            r2 = row_of(u) - col_base
            c2 = col_of(u) - col_base
            plan[z.at_kr_tile + k] = u
            plan[z.at_kr_dst + k] = r2
            plan[z.at_kr_src + k] = c2
            plan[z.at_counts + N_KR] = k + 1

            @pl.loop(0, rt)
            def _(r):
                plan[z.at_need + r * wide + c2] = 1
                plan[z.at_touch + r * ct + r2] = 1

        return 0

    lax.fori_loop(0, n_right, one_kr, 0)

    def sends(t, _):
        r, c, op = row_of(t), col_of(t), op_of(t)
        over_row = (r == row_base - 1) & (c == row_base)
        over_col = (r == col_base - 1) & (c == col_base)

        @pl.when(over_row)
        def _():
            @pl.when(op == NOPS)
            def _():
                @pl.loop(0, ct)
                def _(k):
                    plan[z.at_send_row + k] = 1

            @pl.when(op != NOPS)
            def _():
                @pl.loop(0, n_right)
                def _(b):
                    u = rlist[b]
                    c2 = col_of(u) - col_base

                    @pl.when((op_of(u) == op) & (c2 < ct))
                    def _():
                        plan[z.at_send_row + c2] = 1

                @pl.loop(0, z.total)
                def _(u):
                    @pl.when(
                        (op_of(u) == op)
                        & (row_of(u) == col_base - 1)
                        & (col_of(u) == col_base)
                    )
                    def _():
                        plan[z.at_send_corner] = 1

        @pl.when(over_col)
        def _():
            @pl.when(op == NOPS)
            def _():
                @pl.loop(0, rt)
                def _(k):
                    plan[z.at_send_col + k] = 1

            @pl.when(op != NOPS)
            def _():
                @pl.loop(0, n_left)
                def _(a):
                    u = llist[a]
                    c1 = col_of(u) - row_base

                    @pl.when((op_of(u) == op) & (c1 < rt))
                    def _():
                        plan[z.at_send_col + c1] = 1

        return 0

    lax.fori_loop(0, z.total, sends, 0)


def make_plan(z, here, meta):
    return pl.pallas_call(
        functools.partial(plan_kernel, z),
        out_shape=jax.ShapeDtypeStruct((z.plan_size,), jnp.int32),
        in_specs=[SMEM, SMEM],
        out_specs=SMEM,
        scratch_shapes=[
            pltpu.SMEM((z.total,), jnp.int32),
            pltpu.SMEM((z.total,), jnp.int32),
            pltpu.SMEM((z.total,), jnp.int32),
        ],
        name="plan",
    )(here, meta)


def block_at(z, ref, r, c):
    return ref.at[
        :,
        pl.ds(pl.multiple_of(r * z.edge, z.edge), z.edge),
        pl.ds(pl.multiple_of(c * z.edge, z.edge), z.edge),
    ]


def pack_kernel(z, plan, base, changed, row_buf, col_buf, corner_buf, sem):
    def send(r, c, target):
        touched = plan[z.at_touch + r * z.ct + c] == 1

        @pl.when(touched)
        def _():
            pltpu.make_async_copy(block_at(z, changed, r, c), target, sem).start()

        @pl.when(jnp.logical_not(touched))
        def _():
            pltpu.make_async_copy(block_at(z, base, r, c), target, sem).start()

    def over_row(c, n):
        wanted = plan[z.at_send_row + c] == 1

        @pl.when(wanted)
        def _():
            send(0, c, row_buf.at[n])

        return n + wanted.astype(jnp.int32)

    def over_col(r, n):
        wanted = plan[z.at_send_col + r] == 1

        @pl.when(wanted)
        def _():
            send(r, 0, col_buf.at[n])

        return n + wanted.astype(jnp.int32)

    count = lax.fori_loop(0, z.ct, over_row, jnp.int32(0))
    count = count + lax.fori_loop(0, z.rt, over_col, jnp.int32(0))

    @pl.when(plan[z.at_send_corner] == 1)
    def _():
        send(0, 0, corner_buf.at[0])

    @pl.loop(0, count + plan[z.at_send_corner])
    def _(k):
        pltpu.make_async_copy(block_at(z, base, 0, 0), corner_buf.at[0], sem).wait()


def exchange(z, plan, kind, base, changed):
    def branch(row_slots, col_slots):
        def run(plan, base, changed):
            block = (2, z.edge, z.edge)
            shapes = [(n,) + block for n in (row_slots, col_slots, 1)]
            row_buf, col_buf, corner_buf = pl.pallas_call(
                functools.partial(pack_kernel, z),
                out_shape=[jax.ShapeDtypeStruct(s, jnp.float32) for s in shapes],
                in_specs=[SMEM, ANY, ANY],
                out_specs=[ANY, ANY, ANY],
                scratch_shapes=[pltpu.SemaphoreType.DMA],
                name="pack",
            )(plan, base, changed)
            n, m = z.row_total, z.col_total
            row_in = lax.ppermute(row_buf, "row", [(i + 1, i) for i in range(n - 1)])
            col_in = lax.ppermute(col_buf, "col", [(j + 1, j) for j in range(m - 1)])
            corner_in = lax.ppermute(
                corner_buf,
                BOTH,
                [
                    ((i + 1) * m + j + 1, i * m + j)
                    for i in range(n - 1)
                    for j in range(m - 1)
                ],
            )
            row_in = jnp.pad(row_in, ((0, z.ct - row_slots), (0, 0), (0, 0), (0, 0)))
            col_in = jnp.pad(col_in, ((0, z.rt - col_slots), (0, 0), (0, 0), (0, 0)))
            return row_in, col_in, corner_in

        return run

    return lax.switch(kind, [branch(a, b) for a, b in classes(z)], plan, base, changed)


def classes(z):
    out, slots = [], 2
    while True:
        out.append((min(slots, z.ct), min(slots, z.rt)))
        if slots >= max(z.ct, z.rt):
            return out
        slots *= 2


def class_of(z, rows, cols, ops):
    jump = ops < NOPS
    same = (ops[:, None] == ops[None, :]) & jump[:, None]
    row_slab = rows // z.rt
    col_slab = rows // z.ct
    over_row = (cols != rows) & (cols % z.rt == 0)
    over_col = (cols != rows) & (cols % z.ct == 0)
    in_row = row_slab[:, None] == jnp.arange(z.row_total)[None, :]
    in_col = col_slab[:, None] == jnp.arange(z.col_total)[None, :]

    def worst(over, own, other, full):
        hits = jnp.sum(same[:, :, None] & other[None, :, :], axis=1, dtype=jnp.int32)
        hits = jnp.where(jump[:, None], hits, full)
        picked = (over[:, None] & own)[:, :, None]
        return jnp.max(
            jnp.sum(jnp.where(picked, hits[:, None, :], 0), axis=0, dtype=jnp.int32)
        )

    row_most = worst(over_row, in_row, in_col, z.ct)
    col_most = worst(over_col, in_col, in_row, z.rt)
    kind = jnp.int32(0)
    for row_slots, col_slots in classes(z)[:-1]:
        short = (jnp.minimum(row_most, z.ct) > row_slots) | (
            jnp.minimum(col_most, z.rt) > col_slots
        )
        kind = kind + short.astype(jnp.int32)
    return kind


def halves(x):
    high = x.astype(jnp.bfloat16)
    return high, (x - high.astype(jnp.float32)).astype(jnp.bfloat16)


def dot(a, b):
    return jnp.dot(a, b, preferred_element_type=jnp.float32)


def dot3(a, b):
    return dot(a[0], b[0]) + (dot(a[0], b[1]) + dot(a[1], b[0]))


def stage_kernel(
    z, scale, plan, tiles, base, changed, row_in, col_in, corner_in, *rest
):
    out, cur, acc, lefts, rights, ring, ring_sem, cur_sem, acc_sem, out_sem = rest[-10:]
    rt, ct, wide, edge = z.rt, z.ct, z.wide, z.edge
    second = changed is not base

    def load(src, b):
        pltpu.make_async_copy(src, cur.at[b], cur_sem).start()

    def load_own(k, n):
        r, c = k // ct, k % ct
        b = r * wide + c
        wanted = plan[z.at_need + b] == 1
        touched = plan[z.at_touch + k] == 1

        @pl.when(touched)
        def _():
            pltpu.make_async_copy(block_at(z, base, r, c), acc.at[k], acc_sem).start()

        if second:

            @pl.when(wanted & touched)
            def _():
                load(block_at(z, changed, r, c), b)

            @pl.when(wanted & jnp.logical_not(touched))
            def _():
                load(block_at(z, base, r, c), b)

        else:

            @pl.when(wanted)
            def _():
                load(block_at(z, base, r, c), b)

        return n[0] + wanted.astype(jnp.int32), n[1] + touched.astype(jnp.int32)

    def load_row(c, n):
        b = rt * wide + c
        wanted = plan[z.at_need + b] == 1

        @pl.when(wanted)
        def _():
            load(row_in.at[n], b)

        return n + wanted.astype(jnp.int32)

    def load_col(r, n):
        b = r * wide + ct
        wanted = plan[z.at_need + b] == 1

        @pl.when(wanted)
        def _():
            load(col_in.at[n], b)

        return n + wanted.astype(jnp.int32)

    n_left = plan[z.at_counts + N_LEFT]
    n_right = plan[z.at_counts + N_RIGHT]
    n_kl = plan[z.at_counts + N_KL]
    n_kr = plan[z.at_counts + N_KR]
    n_pair = plan[z.at_counts + N_PAIR]

    def prepare(count, at_tile, build):
        def fetch(k):
            s = k % RING
            tile = plan[at_tile + k]
            return pltpu.make_async_copy(tiles.at[tile], ring.at[s], ring_sem.at[s])

        @pl.loop(0, jnp.minimum(count, RING))
        def _(k):
            fetch(k).start()

        @pl.loop(0, count)
        def _(k):
            fetch(k).wait()
            build(k, ring[k % RING, 0], ring[k % RING, 1])

            @pl.when(k + RING < count)
            def _():
                fetch(k + RING).start()

    def keep(store, k, quads):
        (a, b), (c, d) = quads
        for row, pair in enumerate(((a, b), (c, d))):
            for col, quad in enumerate(pair):
                high, low = halves(quad)
                where = (
                    pl.ds(row * edge, edge),
                    pl.ds(col * edge, edge),
                )
                store[k, 0, where[0], where[1]] = high
                store[k, 1, where[0], where[1]] = low

    def build_left(k, re, im):
        keep(lefts, k, ((re, -im), (im, re)))

    def build_kl(k, re, im):
        re, im = re * scale, im * scale
        keep(lefts, z.left_max + k, ((im, re), (-re, im)))

    def build_right(k, re, im):
        re, im = (re * scale).T, (im * scale).T
        keep(rights, k, ((re, -im), (im, re)))

    def build_kr(k, re, im):
        re, im = (re * scale).T, (im * scale).T
        keep(rights, z.right_max + k, ((im, re), (-re, im)))

    n_cur, n_acc = lax.fori_loop(
        0, rt * ct, load_own, (jnp.int32(0), jnp.int32(0))
    )
    n_cur = n_cur + lax.fori_loop(0, ct, load_row, jnp.int32(0))
    n_cur = n_cur + lax.fori_loop(0, rt, load_col, jnp.int32(0))
    corner = plan[z.at_need + rt * wide + ct]

    @pl.when(corner == 1)
    def _():
        load(corner_in.at[0], rt * wide + ct)

    prepare(n_kl, z.at_kl_tile, build_kl)
    prepare(n_kr, z.at_kr_tile, build_kr)
    prepare(n_left, z.at_left_tile, build_left)
    prepare(n_right, z.at_right_tile, build_right)

    @pl.loop(0, n_cur + corner)
    def _(k):
        pltpu.make_async_copy(row_in.at[0], cur.at[0], cur_sem).wait()

    @pl.loop(0, n_acc)
    def _(k):
        pltpu.make_async_copy(row_in.at[0], acc.at[0], acc_sem).wait()

    def left_times(slot, block):
        x = halves(cur[block].reshape(2 * edge, edge))
        return dot3((lefts[slot, 0], lefts[slot, 1]), x)

    def times_right(product, slot):
        y = halves(jnp.concatenate([product[:edge], product[edge:]], axis=1))
        return dot3(y, (rights[slot, 0], rights[slot, 1]))

    def add_wide(block, product):
        acc[block, 0] += product[:, :edge]
        acc[block, 1] += product[:, edge:]

    @pl.loop(0, n_kl)
    def _(q):
        dst = plan[z.at_kl_dst + q]
        src = plan[z.at_kl_src + q]

        @pl.loop(0, ct // UNROLL)
        def _(g):
            cols = [g * UNROLL + u for u in range(UNROLL)]
            parts = [left_times(z.left_max + q, src + c) for c in cols]
            for c, part in zip(cols, parts):
                acc[dst + c] += part.reshape(2, edge, edge)

    @pl.loop(0, n_kr)
    def _(q):
        dst = plan[z.at_kr_dst + q]
        src = plan[z.at_kr_src + q]

        @pl.loop(0, rt // UNROLL)
        def _(g):
            rows = [g * UNROLL + u for u in range(UNROLL)]
            parts = [
                times_right(cur[r * wide + src].reshape(2 * edge, edge), z.right_max + q)
                for r in rows
            ]
            for r, part in zip(rows, parts):
                add_wide(r * ct + dst, part)

    @pl.loop(0, (n_pair + UNROLL - 1) // UNROLL)
    def _(g):
        spots = [g * UNROLL + u for u in range(UNROLL)]
        firsts = [
            left_times(plan[z.at_pair_left + p], plan[z.at_pair_src + p]) for p in spots
        ]
        parts = [
            times_right(first, plan[z.at_pair_right + p])
            for first, p in zip(firsts, spots)
        ]
        for p, part in zip(spots, parts):
            add_wide(plan[z.at_pair_dst + p], part)

    @pl.loop(0, rt * ct)
    def _(k):
        @pl.when(plan[z.at_touch + k] == 1)
        def _():
            pltpu.make_async_copy(
                acc.at[k], block_at(z, out, k // ct, k % ct), out_sem
            ).start()

    @pl.loop(0, n_acc)
    def _(k):
        pltpu.make_async_copy(acc.at[0], block_at(z, out, 0, 0), out_sem).wait()


def stage(z, scale, plan, tiles, base, changed, halo, result=None):
    block = (2, z.edge, z.edge)
    wide_tile = (2, 2 * z.edge, 2 * z.edge)
    operands = [plan, tiles, base]
    body = functools.partial(stage_kernel, z, scale)
    if changed is None:

        def kernel(plan, tiles, base, *rest):
            body(plan, tiles, base, base, *rest)

    else:
        operands.append(changed)
        kernel = body
    operands.extend(halo)
    aliases = {}
    if result is not None:
        aliases = {len(operands): 0}
        operands.append(result)
    return pl.pallas_call(
        kernel,
        out_shape=jax.ShapeDtypeStruct(base.shape, jnp.float32),
        in_specs=[SMEM] + [ANY] * (len(operands) - 1),
        out_specs=ANY,
        scratch_shapes=[
            pltpu.VMEM(((z.rt + 1) * z.wide,) + block, jnp.float32),
            pltpu.VMEM((z.rt * z.ct + 1,) + block, jnp.float32),
            pltpu.VMEM((z.left_max + CAP,) + wide_tile, jnp.bfloat16),
            pltpu.VMEM((z.right_max + z.right_op,) + wide_tile, jnp.bfloat16),
            pltpu.VMEM((RING,) + block, jnp.float32),
            pltpu.SemaphoreType.DMA((RING,)),
            pltpu.SemaphoreType.DMA,
            pltpu.SemaphoreType.DMA,
            pltpu.SemaphoreType.DMA,
        ],
        input_output_aliases=aliases,
        compiler_params=pltpu.CompilerParams(vmem_limit_bytes=58 * 1024 * 1024),
        name="stage",
    )(*operands)


def local(state, tile_vals, tile_row, tile_col, tile_op):
    z = Sizes(state, tile_vals)
    meta = jnp.stack([tile_row, tile_col, tile_op])
    spread = jnp.broadcast_to(meta[None], (z.row_total * z.col_total,) + meta.shape)
    gathered = lax.all_to_all(spread, BOTH, 0, 0, tiled=True)
    meta = jnp.swapaxes(gathered, 0, 1).reshape(3, z.total)
    tiles = lax.all_gather(tile_vals, BOTH, axis=0, tiled=True)
    here = jnp.stack([lax.axis_index("row"), lax.axis_index("col")]).astype(jnp.int32)
    plan = make_plan(z, here, meta.reshape(-1))
    kind = class_of(z, meta[0], meta[1], meta[2])
    halo = exchange(z, plan, kind, state, state)
    middle = stage(z, 0.5 * TIME_STEP, plan, tiles, state, None, halo)
    halo = exchange(z, plan, kind, state, middle)
    return stage(z, TIME_STEP, plan, tiles, state, middle, halo, state)


def solution(mesh):
    placed = (
        P(None, "row", "col"),
        P(("row", "col"), None, None, None),
        P(("row", "col")),
        P(("row", "col")),
        P(("row", "col")),
    )
    return jax.shard_map(
        local, mesh=mesh, in_specs=placed, out_specs=P(None, "row", "col"), check_vma=False
    )
```

```python
import functools

import jax
import jax.numpy as jnp
from jax import lax
from jax.experimental import pallas as pl
from jax.experimental.pallas import tpu as pltpu
from jax.sharding import PartitionSpec as P

NOPS = 16
CAP = 2
TIME_STEP = 0.25
UNROLL = 4
RING = 8
SLOTS = 4
BOTH = ("row", "col")
ANY = pl.BlockSpec(memory_space=pl.ANY)
SMEM = pl.BlockSpec(memory_space=pltpu.SMEM)


class Sizes:
    def __init__(self, state, tile_vals):
        self.row_total = lax.axis_size("row")
        self.col_total = lax.axis_size("col")
        self.edge = tile_vals.shape[-1]
        self.own = tile_vals.shape[0]
        self.total = self.own * self.row_total * self.col_total
        self.rt = state.shape[1] // self.edge
        self.ct = state.shape[2] // self.edge
        self.span = self.ct // self.rt
        self.left_max = CAP * self.row_total
        self.right_max = self.span * self.left_max
        self.right_op = self.span * CAP
        self.pair_max = self.left_max * self.right_op
        self.pair_pad = -(-self.pair_max // UNROLL) * UNROLL
        self.blocks = self.rt * self.ct
        self.halo_row = self.blocks
        self.halo_col = self.blocks + self.ct
        self.corner = self.blocks + self.ct + self.rt
        self.row_slots = min(SLOTS, self.ct)
        self.col_slots = min(SLOTS, self.rt)
        place = 0
        for name, length in (
            ("counts", 16),
            ("left_tile", self.left_max),
            ("right_tile", self.right_max),
            ("kl_tile", CAP),
            ("kl_dst", CAP),
            ("kl_src", CAP),
            ("kr_tile", self.right_op),
            ("kr_dst", self.right_op),
            ("kr_src", self.right_op),
            ("own_left", self.pair_pad),
            ("own_right", self.pair_pad),
            ("own_src", self.pair_pad),
            ("own_dst", self.pair_pad),
            ("far_left", self.pair_pad),
            ("far_right", self.pair_pad),
            ("far_src", self.pair_pad),
            ("far_dst", self.pair_pad),
            ("read", self.blocks),
            ("hit_own", self.blocks),
            ("hit_far", self.blocks),
            ("hit_all", self.blocks),
            ("hit", self.blocks),
            ("send_row", self.ct),
            ("send_col", self.rt),
            ("take_row", self.ct),
            ("take_col", self.rt),
        ):
            setattr(self, "at_" + name, place)
            place += length
        self.plan_size = -(-place // 128) * 128
        place = 0
        for name, length in (
            ("need", self.corner + 1),
            ("to_row", self.ct),
            ("to_col", self.rt),
        ):
            setattr(self, "flag_" + name, place)
            place += length
        self.flag_size = place


(
    N_LEFT,
    N_RIGHT,
    N_KL,
    N_KR,
    N_OWN,
    N_FAR,
    N_READ,
    N_HIT_OWN,
    N_HIT_FAR,
    N_HIT_ALL,
    N_SEND_ROW,
    N_SEND_COL,
    N_SEND_CORNER,
    N_TAKE_ROW,
    N_TAKE_COL,
    N_TAKE_CORNER,
) = range(16)
OWN, FAR = 1, 2


def plan_kernel(z, here, meta, plan, rlist, llist, slot, flag):
    me_row, me_col = here[0], here[1]
    rt, ct = z.rt, z.ct
    row_base = me_row * rt
    col_base = me_col * ct

    def row_of(t):
        return meta[t]

    def col_of(t):
        return meta[z.total + t]

    def op_of(t):
        return meta[2 * z.total + t]

    @pl.loop(0, 16)
    def _(k):
        plan[k] = 0

    @pl.loop(0, z.blocks)
    def _(k):
        plan[z.at_hit + k] = 0

    @pl.loop(0, z.flag_size)
    def _(k):
        flag[k] = 0

    def push(counter, at_list, value):
        k = plan[counter]
        plan[at_list + k] = value
        plan[counter] = k + 1

    def read(block):
        @pl.when(flag[z.flag_need + block] == 0)
        def _():
            flag[z.flag_need + block] = 1

            @pl.when(block < z.blocks)
            def _():
                push(N_READ, z.at_read, block)

    def write(block, kind):
        old = plan[z.at_hit + block]

        @pl.when((old & kind) == 0)
        def _():
            plan[z.at_hit + block] = old | kind

            @pl.when(old == 0)
            def _():
                push(N_HIT_ALL, z.at_hit_all, block)

            @pl.when(kind == OWN)
            def _():
                push(N_HIT_OWN, z.at_hit_own, block)

            @pl.when(kind == FAR)
            def _():
                push(N_HIT_FAR, z.at_hit_far, block)

    def block_id(r, c):
        inside = jnp.where(c < ct, r * ct + c, z.halo_col + r)
        outside = jnp.where(c < ct, z.halo_row + c, z.corner)
        return jnp.where(r < rt, inside, outside)

    def gather(t, found):
        n_left, n_right = found
        r = row_of(t)
        is_left = (r >= row_base) & (r < row_base + rt)
        is_right = (r >= col_base) & (r < col_base + ct)

        @pl.when(is_left)
        def _():
            llist[n_left] = t

        @pl.when(is_right)
        def _():
            rlist[n_right] = t
            slot[n_right] = -1

        return (
            n_left + is_left.astype(jnp.int32),
            n_right + is_right.astype(jnp.int32),
        )

    n_left, n_right = lax.fori_loop(0, z.total, gather, (jnp.int32(0), jnp.int32(0)))

    def one_left(a, _):
        t = llist[a]
        op = op_of(t)
        r1 = row_of(t) - row_base
        c1 = col_of(t) - row_base

        @pl.when(op == NOPS)
        def _():
            k = plan[N_KL]
            plan[z.at_kl_tile + k] = t
            plan[z.at_kl_dst + k] = r1 * ct
            plan[z.at_kl_src + k] = c1 * ct
            plan[N_KL] = k + 1
            kind = jnp.where(c1 < rt, OWN, FAR)

            @pl.loop(0, ct)
            def _(c):
                read(c1 * ct + c)
                write(r1 * ct + c, kind)

        @pl.when(op != NOPS)
        def _():
            mine = plan[N_LEFT]

            def one_right(b, found):
                u = rlist[b]
                match = op_of(u) == op

                @pl.when(match)
                def _():
                    @pl.when(slot[b] < 0)
                    def _():
                        slot[b] = plan[N_RIGHT]
                        push(N_RIGHT, z.at_right_tile, u)

                    r2 = row_of(u) - col_base
                    c2 = col_of(u) - col_base
                    own = (c1 < rt) & (c2 < ct)
                    src = block_id(c1, c2)
                    dst = r1 * ct + r2

                    @pl.when(own)
                    def _():
                        k = plan[N_OWN]
                        plan[z.at_own_left + k] = mine
                        plan[z.at_own_right + k] = slot[b]
                        plan[z.at_own_src + k] = src
                        plan[z.at_own_dst + k] = dst
                        plan[N_OWN] = k + 1

                    @pl.when(jnp.logical_not(own))
                    def _():
                        k = plan[N_FAR]
                        plan[z.at_far_left + k] = mine
                        plan[z.at_far_right + k] = slot[b]
                        plan[z.at_far_src + k] = src
                        plan[z.at_far_dst + k] = dst
                        plan[N_FAR] = k + 1

                    read(src)
                    write(dst, jnp.where(own, OWN, FAR))

                return found | match.astype(jnp.int32)

            found = lax.fori_loop(0, n_right, one_right, jnp.int32(0))

            @pl.when(found == 1)
            def _():
                push(N_LEFT, z.at_left_tile, t)

        return 0

    lax.fori_loop(0, n_left, one_left, 0)

    def one_kr(b, _):
        u = rlist[b]

        @pl.when(op_of(u) == NOPS)
        def _():
            k = plan[N_KR]
            r2 = row_of(u) - col_base
            c2 = col_of(u) - col_base
            own = c2 < ct
            plan[z.at_kr_tile + k] = u
            plan[z.at_kr_dst + k] = r2
            plan[z.at_kr_src + k] = jnp.where(own, c2, z.halo_col)
            plan[N_KR] = k + 1
            kind = jnp.where(own, OWN, FAR)

            @pl.loop(0, rt)
            def _(r):
                read(block_id(r, c2))
                write(r * ct + r2, kind)

        return 0

    lax.fori_loop(0, n_right, one_kr, 0)

    for count, side, src in ((N_OWN, "own", 0), (N_FAR, "far", z.halo_row)):
        n = plan[count]

        @pl.loop(n, (n + UNROLL - 1) // UNROLL * UNROLL)
        def _(k):
            plan[getattr(z, "at_" + side + "_left") + k] = 0
            plan[getattr(z, "at_" + side + "_right") + k] = 0
            plan[getattr(z, "at_" + side + "_src") + k] = src
            plan[getattr(z, "at_" + side + "_dst") + k] = z.blocks

    def sends(t, _):
        r, c, op = row_of(t), col_of(t), op_of(t)
        over_row = (r == row_base - 1) & (c == row_base)
        over_col = (r == col_base - 1) & (c == col_base)

        @pl.when(over_row)
        def _():
            @pl.when(op == NOPS)
            def _():
                @pl.loop(0, ct)
                def _(k):
                    flag[z.flag_to_row + k] = 1

            @pl.when(op != NOPS)
            def _():
                @pl.loop(0, n_right)
                def _(b):
                    u = rlist[b]
                    c2 = col_of(u) - col_base

                    @pl.when((op_of(u) == op) & (c2 < ct))
                    def _():
                        flag[z.flag_to_row + c2] = 1

                @pl.loop(0, z.total)
                def _(u):
                    @pl.when(
                        (op_of(u) == op)
                        & (row_of(u) == col_base - 1)
                        & (col_of(u) == col_base)
                    )
                    def _():
                        plan[N_SEND_CORNER] = 1

        @pl.when(over_col)
        def _():
            @pl.when(op == NOPS)
            def _():
                @pl.loop(0, rt)
                def _(k):
                    flag[z.flag_to_col + k] = 1

            @pl.when(op != NOPS)
            def _():
                @pl.loop(0, n_left)
                def _(a):
                    u = llist[a]
                    c1 = col_of(u) - row_base

                    @pl.when((op_of(u) == op) & (c1 < rt))
                    def _():
                        flag[z.flag_to_col + c1] = 1

        return 0

    lax.fori_loop(0, z.total, sends, 0)

    for count, at_list, at_flag, length in (
        (N_SEND_ROW, z.at_send_row, z.flag_to_row, ct),
        (N_SEND_COL, z.at_send_col, z.flag_to_col, rt),
        (N_TAKE_ROW, z.at_take_row, z.flag_need + z.halo_row, ct),
        (N_TAKE_COL, z.at_take_col, z.flag_need + z.halo_col, rt),
    ):

        @pl.loop(0, length)
        def _(k):
            @pl.when(flag[at_flag + k] == 1)
            def _():
                push(count, at_list, k)

    plan[N_TAKE_CORNER] = flag[z.flag_need + z.corner]


def make_plan(z, here, meta):
    return pl.pallas_call(
        functools.partial(plan_kernel, z),
        out_shape=jax.ShapeDtypeStruct((z.plan_size,), jnp.int32),
        in_specs=[SMEM, SMEM],
        out_specs=SMEM,
        scratch_shapes=[
            pltpu.SMEM((z.total,), jnp.int32),
            pltpu.SMEM((z.total,), jnp.int32),
            pltpu.SMEM((z.total,), jnp.int32),
            pltpu.SMEM((z.flag_size,), jnp.int32),
        ],
        name="plan",
    )(here, meta)


def block_at(z, ref, block):
    r, c = block // z.ct, block % z.ct
    return ref.at[
        :,
        pl.ds(pl.multiple_of(r * z.edge, z.edge), z.edge),
        pl.ds(pl.multiple_of(c * z.edge, z.edge), z.edge),
    ]


def start_block(z, plan, base, changed, block, target, sem):
    if changed is None:
        pltpu.make_async_copy(block_at(z, base, block), target, sem).start()
        return
    written = plan[z.at_hit + block] != 0

    @pl.when(written)
    def _():
        pltpu.make_async_copy(block_at(z, changed, block), target, sem).start()

    @pl.when(jnp.logical_not(written))
    def _():
        pltpu.make_async_copy(block_at(z, base, block), target, sem).start()


def pack(z, plan, base, changed, first, row_n, col_n):
    row_lo = 0 if first else z.row_slots
    col_lo = 0 if first else z.col_slots
    lengths = [row_n, max(col_n, 1)] + ([1] if first else [])

    def kernel(plan, *refs):
        base_ref = refs[0]
        changed_ref = refs[1] if changed is not None else None
        outs = refs[-1 - len(lengths) : -1]
        sem = refs[-1]
        n_row = jnp.clip(plan[N_SEND_ROW] - row_lo, 0, row_n)
        n_col = jnp.clip(plan[N_SEND_COL] - col_lo, 0, col_n)
        n_all = n_row + n_col

        @pl.loop(0, n_row)
        def _(k):
            block = plan[z.at_send_row + row_lo + k]
            start_block(z, plan, base_ref, changed_ref, block, outs[0].at[k], sem)

        @pl.loop(0, n_col)
        def _(k):
            block = plan[z.at_send_col + col_lo + k] * z.ct
            start_block(z, plan, base_ref, changed_ref, block, outs[1].at[k], sem)

        if first:
            n_all = n_all + plan[N_SEND_CORNER]

            @pl.when(plan[N_SEND_CORNER] == 1)
            def _():
                start_block(z, plan, base_ref, changed_ref, 0, outs[2].at[0], sem)

        @pl.loop(0, n_all)
        def _(k):
            pltpu.make_async_copy(block_at(z, base_ref, 0), outs[0].at[0], sem).wait()

    operands = [plan, base] + ([changed] if changed is not None else [])
    block = (2, z.edge, z.edge)
    return pl.pallas_call(
        kernel,
        out_shape=[jax.ShapeDtypeStruct((n,) + block, jnp.float32) for n in lengths],
        in_specs=[SMEM] + [ANY] * (len(operands) - 1),
        out_specs=[pl.BlockSpec(memory_space=pltpu.VMEM)] * len(lengths),
        scratch_shapes=[pltpu.SemaphoreType.DMA],
        name="pack",
    )(*operands)


def exchange(z, plan, kind, base, changed):
    n, m = z.row_total, z.col_total
    row_route = [(i + 1, i) for i in range(n - 1)]
    col_route = [(j + 1, j) for j in range(m - 1)]
    both_route = [
        ((i + 1) * m + j + 1, i * m + j) for i in range(n - 1) for j in range(m - 1)
    ]
    first = (z.row_slots, z.col_slots)
    row_buf, col_buf, corner_buf = pack(z, plan, base, changed, True, *first)
    row_in = lax.ppermute(row_buf, "row", row_route)
    col_in = lax.ppermute(col_buf, "col", col_route)
    corner_in = lax.ppermute(corner_buf, BOTH, both_route)
    sizes = extra_sizes(z)
    full = (sizes[-1][0], max(sizes[-1][1], 1))
    if full[0] == 0:
        return row_in, col_in, corner_in

    def run(row_n, col_n):
        def branch(plan, base, changed):
            row_buf, col_buf = pack(z, plan, base, changed, False, row_n, col_n)
            moved = (
                lax.ppermute(row_buf, "row", row_route),
                lax.ppermute(col_buf, "col", col_route),
            )
            return tuple(
                jnp.pad(x, ((0, n - x.shape[0]), (0, 0), (0, 0), (0, 0)))
                for x, n in zip(moved, full)
            )

        return branch

    def skip(plan, base, changed):
        def kernel(plan, *outs):
            pass

        block = (2, z.edge, z.edge)
        return tuple(
            pl.pallas_call(
                kernel,
                out_shape=[jax.ShapeDtypeStruct((n,) + block, jnp.float32) for n in full],
                in_specs=[SMEM],
                out_specs=[ANY, ANY],
                name="skip",
            )(plan)
        )

    branches = [skip] + [run(*size) for size in sizes]
    rest = lax.switch(kind, branches, plan, base, changed)
    return row_in, col_in, corner_in, *rest


def extra_kind(z, rows, cols, ops):
    jump = ops < NOPS
    same = (ops[:, None] == ops[None, :]) & jump[:, None]
    places = jnp.arange(z.row_total * z.rt)

    def most(edge, other, full):
        slab = rows // edge
        over = (cols != rows) & (cols % edge == 0)
        own = slab[:, None] == jnp.arange(places.shape[0] // edge)[None, :]
        picked = over[:, None] & own
        hit = jnp.any(picked[:, None, :] & same[:, :, None], axis=0)
        inside = rows // other == cols // other
        at = (cols[:, None] == places[None, :]) & inside[:, None]
        read = jnp.any(hit[:, :, None] & at[:, None, :], axis=0)
        counts = jnp.sum(
            read.reshape(read.shape[0], -1, other), axis=2, dtype=jnp.int32
        )
        whole = jnp.any(over & (ops == NOPS))
        return jnp.maximum(jnp.max(counts), jnp.where(whole, full, 0))

    row_most = most(z.rt, z.ct, z.ct)
    col_most = most(z.ct, z.rt, z.rt)
    kind = jnp.int32(0)
    for row_slots, col_slots in [(0, 0)] + extra_sizes(z)[:-1]:
        short = (row_most > z.row_slots + row_slots) | (
            col_most > z.col_slots + col_slots
        )
        kind = kind + short.astype(jnp.int32)
    return kind


def extra_sizes(z):
    sizes = [
        (min(z.row_slots, z.ct - z.row_slots), min(z.col_slots, z.rt - z.col_slots)),
        (z.ct - z.row_slots, z.rt - z.col_slots),
    ]
    return sizes[:1] if sizes[0] == sizes[1] else sizes


def halves(x):
    high = x.astype(jnp.bfloat16)
    return high, (x - high.astype(jnp.float32)).astype(jnp.bfloat16)


def dot(a, b):
    return jnp.dot(a, b, preferred_element_type=jnp.float32)


def wait_each(count, copy):
    @pl.loop(0, count)
    def _(k):
        copy.wait()


def load_halo(z, plan, halo, cur, shift, sem):
    row_in, col_in, corner_in = halo[:3]
    for count, at_list, start, slots, first, second in (
        (N_TAKE_ROW, z.at_take_row, z.halo_row, z.row_slots, row_in, halo[3:4]),
        (N_TAKE_COL, z.at_take_col, z.halo_col, z.col_slots, col_in, halo[4:5]),
    ):
        n = plan[count]

        @pl.loop(0, jnp.minimum(n, slots))
        def _(k):
            place = cur.at[start + plan[at_list + k] - shift]
            pltpu.make_async_copy(first.at[k], place, sem).start()

        if second:

            @pl.loop(slots, n)
            def _(k):
                place = cur.at[start + plan[at_list + k] - shift]
                pltpu.make_async_copy(second[0].at[k - slots], place, sem).start()

    @pl.when(plan[N_TAKE_CORNER] == 1)
    def _():
        pltpu.make_async_copy(corner_in.at[0], cur.at[z.corner - shift], sem).start()

    return plan[N_TAKE_ROW] + plan[N_TAKE_COL] + plan[N_TAKE_CORNER]


class Work:
    def __init__(self, z, gain, plan, cur, acc, shift):
        self.z, self.gain, self.plan = z, gain, plan
        self.cur, self.acc, self.shift = cur, acc, shift

    def scaled(self, part):
        return part if self.gain == 1 else self.gain * part

    def left_times(self, tile, block):
        edge = self.z.edge
        high, low = halves(self.cur[block - self.shift].reshape(2 * edge, edge))
        both = dot(tile[0], jnp.concatenate([high, low], axis=1))
        return both[:, :edge] + (both[:, edge:] + dot(tile[1], high))

    def times_right(self, y, tile):
        rows = y.shape[0]
        high, low = halves(y)
        both = dot(jnp.concatenate([high, low], axis=0), tile[0])
        return both[:rows] + (both[rows:] + dot(high, tile[1]))

    def flat(self, block):
        value = self.cur[block - self.shift]
        return jnp.concatenate([value[0], value[1]], axis=1)

    def add_wide(self, block, part):
        edge = self.z.edge
        part = self.scaled(part)
        self.acc[block, 0] += part[:, :edge]
        self.acc[block, 1] += part[:, edge:]

    def ham_left(self, q, tile):
        z, edge = self.z, self.z.edge
        dst = self.plan[z.at_kl_dst + q]
        src = self.plan[z.at_kl_src + q]

        @pl.loop(0, z.ct // UNROLL)
        def _(g):
            cols = [g * UNROLL + u for u in range(UNROLL)]
            parts = []
            for a, b in zip(cols[::2], cols[1::2]):
                x = [
                    self.cur[src + c - self.shift].reshape(2 * edge, edge) for c in (a, b)
                ]
                high, low = halves(jnp.concatenate(x, axis=1))
                part = dot(tile[0], high) + (dot(tile[0], low) + dot(tile[1], high))
                parts += [part[:, :edge], part[:, edge:]]
            for c, part in zip(cols, parts):
                self.acc[dst + c] += self.scaled(part.reshape(2, edge, edge))

    def ham_right(self, q, tile, far):
        z, edge = self.z, self.z.edge
        dst = self.plan[z.at_kr_dst + q]
        src = self.plan[z.at_kr_src + q]

        @pl.loop(0, z.rt // UNROLL)
        def _(g):
            rows = [g * UNROLL + u for u in range(UNROLL)]
            y = jnp.concatenate(
                [self.flat(src + (r if far else r * z.ct)) for r in rows], axis=0
            )
            parts = self.times_right(y, tile)
            for u, r in enumerate(rows):
                self.add_wide(r * z.ct + dst, parts[u * edge : (u + 1) * edge])

    def pairs(self, side, g, left_of, right_of):
        z, plan, edge = self.z, self.plan, self.z.edge
        spots = [g * UNROLL + u for u in range(UNROLL)]
        at_src = getattr(z, "at_" + side + "_src")
        at_dst = getattr(z, "at_" + side + "_dst")
        firsts = [
            self.left_times(left_of(u, p), plan[at_src + p]) for u, p in enumerate(spots)
        ]
        parts = [
            self.times_right(
                jnp.concatenate([first[:edge], first[edge:]], axis=1), right_of(u, p)
            )
            for (u, p), first in zip(enumerate(spots), firsts)
        ]
        for p, part in zip(spots, parts):
            self.add_wide(plan[at_dst + p], part)


def store_blocks(z, plan, count, at_list, acc, out, sem):
    n = plan[count]

    @pl.loop(0, n)
    def _(k):
        block = plan[at_list + k]
        pltpu.make_async_copy(acc.at[block], block_at(z, out, block), sem).start()

    wait_each(n, pltpu.make_async_copy(acc.at[0], block_at(z, out, 0), sem))


def load_blocks(z, plan, count, at_list, src, acc, sem):
    @pl.loop(0, plan[count])
    def _(k):
        block = plan[at_list + k]
        pltpu.make_async_copy(block_at(z, src, block), acc.at[block], sem).start()


def groups(n):
    return (n + UNROLL - 1) // UNROLL


def tile_shape(z, count):
    return (count, 2, 2 * z.edge, 2 * z.edge)


SCALE = 0.5 * TIME_STEP


def stage_kernel(z, second, plan, *refs):
    if second:
        lefts_in, rights_in, base, changed, _, out = refs[:6]
        refs = refs[6:]
        halo = None
    else:
        tiles, base = refs[:2]
        halo = refs[2:-12]
        out, lefts_out, rights_out = refs[-11:-8]
        changed = None
        refs = refs[-8:]
    cur, acc, lefts, rights, ring, ring_sem, sems, tile_sem = refs
    cur_sem, acc_sem, out_sem = (sems.at[k] for k in range(3))
    edge = z.edge
    n_left, n_right = plan[N_LEFT], plan[N_RIGHT]
    n_kl, n_kr = plan[N_KL], plan[N_KR]
    n_tiles = n_left + n_right + n_kl + n_kr
    kept = (
        (n_kl, z.left_max, lefts, 0),
        (n_kr, z.right_max, rights, 1),
        (n_left, 0, lefts, 0),
        (n_right, 0, rights, 1),
    )

    if second:
        for count, start, place, which in kept:
            source = (lefts_in, rights_in)[which]

            @pl.loop(0, count)
            def _(k):
                pltpu.make_async_copy(
                    source.at[start + k], place.at[start + k], tile_sem
                ).start()

    n_read = plan[N_READ]

    @pl.loop(0, n_read)
    def _(k):
        block = plan[z.at_read + k]
        start_block(z, plan, base, changed, block, cur.at[block], cur_sem)

    hits = (N_HIT_OWN, z.at_hit_own) if second else (N_HIT_ALL, z.at_hit_all)
    load_blocks(z, plan, *hits, base, acc, acc_sem)

    if second:
        wait_each(
            n_tiles, pltpu.make_async_copy(lefts_in.at[0], lefts.at[0], tile_sem)
        )
    else:
        n_read = n_read + load_halo(z, plan, halo, cur, 0, cur_sem)

        def prepare(count, at_tile, start, place, target, build):
            def fetch(k):
                s = k % RING
                tile = plan[at_tile + k]
                return pltpu.make_async_copy(tiles.at[tile], ring.at[s], ring_sem.at[s])

            @pl.loop(0, jnp.minimum(count, RING))
            def _(k):
                fetch(k).start()

            @pl.loop(0, count)
            def _(k):
                fetch(k).wait()
                quads = build(ring[k % RING, 0], ring[k % RING, 1])
                for part in (0, 1):
                    for row in (0, 1):
                        for col in (0, 1):
                            place[
                                start + k,
                                part,
                                row * edge : (row + 1) * edge,
                                col * edge : (col + 1) * edge,
                            ] = quads[row][col][part]
                pltpu.make_async_copy(
                    place.at[start + k], target.at[start + k], tile_sem
                ).start()

                @pl.when(k + RING < count)
                def _():
                    fetch(k + RING).start()

        def plain(re, im):
            minus = tuple(-part for part in im)
            return ((re, minus), (im, re))

        def turned(re, im):
            minus = tuple(-part for part in re)
            return ((im, re), (minus, im))

        def build_left(re, im):
            return plain(halves(re), halves(im))

        def build_right(re, im):
            return plain(halves((re * SCALE).T), halves((im * SCALE).T))

        def build_kr(re, im):
            return turned(halves((re * SCALE).T), halves((im * SCALE).T))

        def build_kl(re, im):
            return turned(halves(re * SCALE), halves(im * SCALE))

        prepare(n_kl, z.at_kl_tile, z.left_max, lefts, lefts_out, build_kl)
        prepare(n_kr, z.at_kr_tile, z.right_max, rights, rights_out, build_kr)
        prepare(n_left, z.at_left_tile, 0, lefts, lefts_out, build_left)
        prepare(n_right, z.at_right_tile, 0, rights, rights_out, build_right)

    wait_each(n_read, pltpu.make_async_copy(block_at(z, base, 0), cur.at[0], cur_sem))
    wait_each(
        plan[hits[0]], pltpu.make_async_copy(block_at(z, base, 0), acc.at[0], acc_sem)
    )
    work = Work(z, 2 if second else 1, plan, cur, acc, 0)

    def tile_of(store, slot):
        return store[slot, 0], store[slot, 1]

    @pl.loop(0, n_kl)
    def _(q):
        far = plan[z.at_kl_src + q] >= z.blocks

        @pl.when(jnp.logical_not(far) if second else True)
        def _():
            work.ham_left(q, tile_of(lefts, z.left_max + q))

    @pl.loop(0, n_kr)
    def _(q):
        far = plan[z.at_kr_src + q] >= z.blocks
        tile = tile_of(rights, z.right_max + q)

        @pl.when(jnp.logical_not(far))
        def _():
            work.ham_right(q, tile, False)

        if not second:

            @pl.when(far)
            def _():
                work.ham_right(q, tile, True)

    for count, side in ((N_OWN, "own"), (N_FAR, "far"))[: 1 if second else 2]:
        at_left = getattr(z, "at_" + side + "_left")
        at_right = getattr(z, "at_" + side + "_right")

        @pl.loop(0, groups(plan[count]))
        def _(g):
            work.pairs(
                side,
                g,
                lambda u, p: tile_of(lefts, plan[at_left + p]),
                lambda u, p: tile_of(rights, plan[at_right + p]),
            )

    store_blocks(z, plan, *hits, acc, out, out_sem)
    if not second:
        wait_each(
            n_tiles, pltpu.make_async_copy(lefts.at[0], lefts_out.at[0], tile_sem)
        )


def far_kernel(z, n_halo, plan, lefts_in, rights_in, result, *refs):
    halo = refs[:n_halo]
    out, cur, acc, lefts, rights, sems = refs[n_halo:]
    cur_sem, acc_sem, out_sem, tile_sem = (sems.at[k] for k in range(4))
    n_read = load_halo(z, plan, halo, cur, z.blocks, cur_sem)
    load_blocks(z, plan, N_HIT_FAR, z.at_hit_far, result, acc, acc_sem)
    wait_each(n_read, pltpu.make_async_copy(halo[2].at[0], cur.at[0], cur_sem))
    wait_each(
        plan[N_HIT_FAR],
        pltpu.make_async_copy(block_at(z, result, 0), acc.at[0], acc_sem),
    )
    work = Work(z, 2, plan, cur, acc, z.blocks)

    def bring(slot, source, place):
        copy = pltpu.make_async_copy(source.at[slot], place, tile_sem)
        copy.start()
        return copy

    @pl.loop(0, groups(plan[N_FAR]))
    def _(g):
        copies = []
        for u in range(UNROLL):
            p = g * UNROLL + u
            copies.append(bring(plan[z.at_far_left + p], lefts_in, lefts.at[u]))
            copies.append(bring(plan[z.at_far_right + p], rights_in, rights.at[u]))
        for copy in copies:
            copy.wait()
        work.pairs(
            "far",
            g,
            lambda u, p: (lefts[u, 0], lefts[u, 1]),
            lambda u, p: (rights[u, 0], rights[u, 1]),
        )

    @pl.loop(0, plan[N_KL])
    def _(q):
        @pl.when(plan[z.at_kl_src + q] >= z.blocks)
        def _():
            bring(z.left_max + q, lefts_in, lefts.at[0]).wait()
            work.ham_left(q, (lefts[0, 0], lefts[0, 1]))

    @pl.loop(0, plan[N_KR])
    def _(q):
        @pl.when(plan[z.at_kr_src + q] >= z.blocks)
        def _():
            bring(z.right_max + q, rights_in, rights.at[0]).wait()
            work.ham_right(q, (rights[0, 0], rights[0, 1]), True)

    store_blocks(z, plan, N_HIT_FAR, z.at_hit_far, acc, out, out_sem)


PARAMS = pltpu.CompilerParams(vmem_limit_bytes=58 * 1024 * 1024)


def copy_of(z, base):
    spec = pl.BlockSpec((2, z.edge, base.shape[2]), lambda r: (0, r, 0))

    def kernel(src, dst):
        dst[...] = src[...]

    return pl.pallas_call(
        kernel,
        out_shape=jax.ShapeDtypeStruct(base.shape, jnp.float32),
        grid=(z.rt,),
        in_specs=[spec],
        out_specs=spec,
        name="copy_of",
    )(base)


def first_stage(z, plan, tiles, base, halo, result):
    block = (2, z.edge, z.edge)
    lefts = tile_shape(z, z.left_max + CAP)
    rights = tile_shape(z, z.right_max + z.right_op)
    return pl.pallas_call(
        functools.partial(stage_kernel, z, False),
        out_shape=[
            jax.ShapeDtypeStruct(base.shape, jnp.float32),
            jax.ShapeDtypeStruct(lefts, jnp.bfloat16),
            jax.ShapeDtypeStruct(rights, jnp.bfloat16),
        ],
        in_specs=[SMEM] + [ANY] * (3 + len(halo)),
        out_specs=[ANY] * 3,
        scratch_shapes=[
            pltpu.VMEM((z.corner + 1,) + block, jnp.float32),
            pltpu.VMEM((z.blocks + 1,) + block, jnp.float32),
            pltpu.VMEM(lefts, jnp.bfloat16),
            pltpu.VMEM(rights, jnp.bfloat16),
            pltpu.VMEM((RING,) + block, jnp.float32),
            pltpu.SemaphoreType.DMA((RING,)),
            pltpu.SemaphoreType.DMA((3,)),
            pltpu.SemaphoreType.DMA,
        ],
        compiler_params=PARAMS,
        cost_estimate=COST,
        name="stage_one",
    )(plan, tiles, base, *halo, result)


COST = pl.CostEstimate(flops=4_000_000_000, bytes_accessed=48_000_000, transcendentals=0)


def second_stage(z, plan, lefts, rights, base, middle, result):
    block = (2, z.edge, z.edge)
    return pl.pallas_call(
        functools.partial(stage_kernel, z, True),
        out_shape=jax.ShapeDtypeStruct(base.shape, jnp.float32),
        in_specs=[SMEM] + [ANY] * 5,
        out_specs=ANY,
        scratch_shapes=[
            pltpu.VMEM((z.blocks,) + block, jnp.float32),
            pltpu.VMEM((z.blocks + 1,) + block, jnp.float32),
            pltpu.VMEM(lefts.shape, jnp.bfloat16),
            pltpu.VMEM(rights.shape, jnp.bfloat16),
            pltpu.VMEM((1,) + block, jnp.float32),
            pltpu.SemaphoreType.DMA((1,)),
            pltpu.SemaphoreType.DMA((3,)),
            pltpu.SemaphoreType.DMA,
        ],
        input_output_aliases={5: 0},
        compiler_params=PARAMS,
        cost_estimate=COST,
        name="stage_two",
    )(plan, lefts, rights, base, middle, result)


def far_stage(z, plan, lefts, rights, result, halo):
    block = (2, z.edge, z.edge)
    return pl.pallas_call(
        functools.partial(far_kernel, z, len(halo)),
        out_shape=jax.ShapeDtypeStruct(result.shape, jnp.float32),
        in_specs=[SMEM] + [ANY] * (3 + len(halo)),
        out_specs=ANY,
        scratch_shapes=[
            pltpu.VMEM((z.corner + 1 - z.blocks,) + block, jnp.float32),
            pltpu.VMEM((z.blocks + 1,) + block, jnp.float32),
            pltpu.VMEM(tile_shape(z, UNROLL), jnp.bfloat16),
            pltpu.VMEM(tile_shape(z, UNROLL), jnp.bfloat16),
            pltpu.SemaphoreType.DMA((4,)),
        ],
        input_output_aliases={3: 0},
        compiler_params=PARAMS,
        name="far",
    )(plan, lefts, rights, result, *halo)


def local(state, tile_vals, tile_row, tile_col, tile_op):
    z = Sizes(state, tile_vals)
    meta = jnp.stack([tile_row, tile_col, tile_op])
    spread = jnp.broadcast_to(meta[None], (z.row_total * z.col_total,) + meta.shape)
    gathered = lax.all_to_all(spread, BOTH, 0, 0, tiled=True)
    meta = jnp.swapaxes(gathered, 0, 1).reshape(3, z.total)
    tiles = lax.all_gather(tile_vals, BOTH, axis=0, tiled=True)
    here = jnp.stack([lax.axis_index("row"), lax.axis_index("col")]).astype(jnp.int32)
    plan = make_plan(z, here, meta.reshape(-1))
    kind = extra_kind(z, meta[0], meta[1], meta[2])
    halo = exchange(z, plan, kind, state, None)
    result = copy_of(z, state)
    middle, lefts, rights = first_stage(z, plan, tiles, state, halo, result)
    halo = exchange(z, plan, kind, state, middle)
    result = second_stage(z, plan, lefts, rights, state, middle, result)
    return far_stage(z, plan, lefts, rights, result, halo)


def solution(mesh):
    placed = (
        P(None, "row", "col"),
        P(("row", "col"), None, None, None),
        P(("row", "col")),
        P(("row", "col")),
        P(("row", "col")),
    )
    return jax.shard_map(
        local, mesh=mesh, in_specs=placed, out_specs=P(None, "row", "col"), check_vma=False
    )
```

```python
import functools

import jax
import jax.numpy as jnp
from jax import lax
from jax.experimental import pallas as pl
from jax.experimental.pallas import tpu as pltpu
from jax.sharding import PartitionSpec as P

NOPS = 16
CAP = 2
TIME_STEP = 0.25
UNROLL = 4
RING = 8
SLOTS = 4
PLACES = 1024
BOTH = ("row", "col")
ANY = pl.BlockSpec(memory_space=pl.ANY)
SMEM = pl.BlockSpec(memory_space=pltpu.SMEM)


class Sizes:
    def __init__(self, state, tile_vals):
        self.row_total = lax.axis_size("row")
        self.col_total = lax.axis_size("col")
        self.edge = tile_vals.shape[-1]
        self.own = tile_vals.shape[0]
        self.total = self.own * self.row_total * self.col_total
        self.rt = state.shape[1] // self.edge
        self.ct = state.shape[2] // self.edge
        self.span = self.ct // self.rt
        self.left_max = CAP * self.row_total
        self.right_max = self.span * self.left_max
        self.right_op = self.span * CAP
        self.pair_max = self.left_max * self.right_op
        self.pair_pad = -(-self.pair_max // UNROLL) * UNROLL
        self.blocks = self.rt * self.ct
        self.halo_row = self.blocks
        self.halo_col = self.blocks + self.ct
        self.corner = self.blocks + self.ct + self.rt
        self.row_slots = min(SLOTS, self.ct)
        self.col_slots = min(SLOTS, self.rt)
        place = 0
        for name, length in (
            ("counts", 16),
            ("left_tile", self.left_max),
            ("right_tile", self.right_max),
            ("kl_tile", CAP),
            ("kl_dst", CAP),
            ("kl_src", CAP),
            ("kr_tile", self.right_op),
            ("kr_dst", self.right_op),
            ("kr_src", self.right_op),
            ("own_left", self.pair_pad),
            ("own_right", self.pair_pad),
            ("own_src", self.pair_pad),
            ("own_dst", self.pair_pad),
            ("far_left", self.pair_pad),
            ("far_right", self.pair_pad),
            ("far_src", self.pair_pad),
            ("far_dst", self.pair_pad),
            ("read", self.blocks),
            ("hit_own", self.blocks),
            ("hit_far", self.blocks),
            ("hit_all", self.blocks),
            ("hit", self.blocks),
            ("send_row", self.ct),
            ("send_col", self.rt),
            ("take_row", self.ct),
            ("take_col", self.rt),
        ):
            setattr(self, "at_" + name, place)
            place += length
        self.plan_size = -(-place // 128) * 128
        self.by_hops = (self.row_total, self.col_total) == (8, 4)
        self.arrays = 6 if self.by_hops else 1
        place = 0
        for name, length in (
            ("need", self.corner + 1),
            ("to_row", self.ct),
            ("to_col", self.rt),
        ):
            setattr(self, "flag_" + name, place)
            place += length
        self.flag_size = place


    def tile_place(self, tile, here):
        if not self.by_hops:
            return tile
        device = tile // self.own
        row = (device // self.col_total) ^ here[0]
        col = (device % self.col_total) ^ here[1]
        hop = here[2 + ((row // 2) * 4 + ((row & 1) | (col & 2)))]
        array = hop // PLACES + (col & 1) * 3
        return array * PLACES + (hop % PLACES) * self.own + tile % self.own


(
    N_LEFT,
    N_RIGHT,
    N_KL,
    N_KR,
    N_OWN,
    N_FAR,
    N_READ,
    N_HIT_OWN,
    N_HIT_FAR,
    N_HIT_ALL,
    N_SEND_ROW,
    N_SEND_COL,
    N_SEND_CORNER,
    N_TAKE_ROW,
    N_TAKE_COL,
    N_TAKE_CORNER,
) = range(16)
OWN, FAR = 1, 2


def plan_kernel(z, here, meta, plan, llist, rows_over, cols_over, slot, flag, by_op, bucket):
    me_row, me_col = here[0], here[1]
    rt, ct = z.rt, z.ct
    row_base = me_row * rt
    col_base = me_col * ct

    def row_of(t):
        return meta[t]

    def col_of(t):
        return meta[z.total + t]

    def op_of(t):
        return meta[2 * z.total + t]

    def clear(ref, start, length):
        step = 8

        @pl.loop(0, length // step)
        def _(k):
            for u in range(step):
                ref[start + k * step + u] = 0

        for k in range(length // step * step, length):
            ref[start + k] = 0

    clear(plan, 0, 16)
    clear(plan, z.at_hit, z.blocks)
    clear(flag, 0, z.flag_size)
    clear(by_op, 0, NOPS + 1)

    def place(tile):
        return z.tile_place(tile, here)

    def push(counter, at_list, value):
        k = plan[counter]
        plan[at_list + k] = value
        plan[counter] = k + 1

    def read(block):
        @pl.when(flag[z.flag_need + block] == 0)
        def _():
            flag[z.flag_need + block] = 1

            @pl.when(block < z.blocks)
            def _():
                push(N_READ, z.at_read, block)

    def write(block, kind):
        old = plan[z.at_hit + block]

        @pl.when((old & kind) == 0)
        def _():
            plan[z.at_hit + block] = old | kind

            @pl.when(old == 0)
            def _():
                push(N_HIT_ALL, z.at_hit_all, block)

            @pl.when(kind == OWN)
            def _():
                push(N_HIT_OWN, z.at_hit_own, block)

            @pl.when(kind == FAR)
            def _():
                push(N_HIT_FAR, z.at_hit_far, block)

    def block_id(r, c):
        inside = jnp.where(c < ct, r * ct + c, z.halo_col + r)
        outside = jnp.where(c < ct, z.halo_row + c, z.corner)
        return jnp.where(r < rt, inside, outside)

    def gather(t, found):
        n_left, n_row, n_col = found
        r, c = row_of(t), col_of(t)
        is_left = (r >= row_base) & (r < row_base + rt)
        over_row = (r == row_base - 1) & (c == row_base)
        over_col = (r == col_base - 1) & (c == col_base)

        @pl.when(is_left)
        def _():
            llist[n_left] = t

        @pl.when((r >= col_base) & (r < col_base + ct))
        def _():
            op = op_of(t)
            k = by_op[op]
            bucket[op * z.right_op + k] = t
            by_op[op] = k + 1
            slot[t] = -1

        @pl.when(over_row)
        def _():
            rows_over[n_row] = t

        @pl.when(over_col)
        def _():
            cols_over[n_col] = t

        return (
            n_left + is_left.astype(jnp.int32),
            n_row + over_row.astype(jnp.int32),
            n_col + over_col.astype(jnp.int32),
        )

    n_left, n_row, n_col = lax.fori_loop(0, z.total, gather, (jnp.int32(0),) * 3)

    def one_left(a, _):
        t = llist[a]
        op = op_of(t)
        r1 = row_of(t) - row_base
        c1 = col_of(t) - row_base

        @pl.when(op == NOPS)
        def _():
            k = plan[N_KL]
            plan[z.at_kl_tile + k] = place(t)
            plan[z.at_kl_dst + k] = r1 * ct
            plan[z.at_kl_src + k] = c1 * ct
            plan[N_KL] = k + 1
            kind = jnp.where(c1 < rt, OWN, FAR)

            @pl.loop(0, ct)
            def _(c):
                read(c1 * ct + c)
                write(r1 * ct + c, kind)

        @pl.when(op != NOPS)
        def _():
            mine = plan[N_LEFT]
            n_match = by_op[op]

            @pl.loop(0, n_match)
            def _(b):
                u = bucket[op * z.right_op + b]

                @pl.when(slot[u] < 0)
                def _():
                    slot[u] = plan[N_RIGHT]
                    push(N_RIGHT, z.at_right_tile, place(u))

                r2 = row_of(u) - col_base
                c2 = col_of(u) - col_base
                own = (c1 < rt) & (c2 < ct)
                src = block_id(c1, c2)
                dst = r1 * ct + r2

                @pl.when(own)
                def _():
                    k = plan[N_OWN]
                    plan[z.at_own_left + k] = mine
                    plan[z.at_own_right + k] = slot[u]
                    plan[z.at_own_src + k] = src
                    plan[z.at_own_dst + k] = dst
                    plan[N_OWN] = k + 1

                @pl.when(jnp.logical_not(own))
                def _():
                    k = plan[N_FAR]
                    plan[z.at_far_left + k] = mine
                    plan[z.at_far_right + k] = slot[u]
                    plan[z.at_far_src + k] = src
                    plan[z.at_far_dst + k] = dst
                    plan[N_FAR] = k + 1

                read(src)
                write(dst, jnp.where(own, OWN, FAR))

            @pl.when(n_match > 0)
            def _():
                push(N_LEFT, z.at_left_tile, place(t))

        return 0

    lax.fori_loop(0, n_left, one_left, 0)

    @pl.loop(0, by_op[NOPS])
    def _(k):
        u = bucket[NOPS * z.right_op + k]
        r2 = row_of(u) - col_base
        c2 = col_of(u) - col_base
        own = c2 < ct
        plan[z.at_kr_tile + k] = place(u)
        plan[z.at_kr_dst + k] = r2
        plan[z.at_kr_src + k] = jnp.where(own, c2, z.halo_col)
        kind = jnp.where(own, OWN, FAR)

        @pl.loop(0, rt)
        def _(r):
            read(block_id(r, c2))
            write(r * ct + r2, kind)

    plan[N_KR] = by_op[NOPS]

    for count, side, src in ((N_OWN, "own", 0), (N_FAR, "far", z.halo_row)):
        n = plan[count]

        @pl.loop(n, (n + UNROLL - 1) // UNROLL * UNROLL)
        def _(k):
            plan[getattr(z, "at_" + side + "_left") + k] = 0
            plan[getattr(z, "at_" + side + "_right") + k] = 0
            plan[getattr(z, "at_" + side + "_src") + k] = src
            plan[getattr(z, "at_" + side + "_dst") + k] = z.blocks

    @pl.loop(0, n_row)
    def _(a):
        op = op_of(rows_over[a])

        @pl.when(op == NOPS)
        def _():
            @pl.loop(0, ct)
            def _(k):
                flag[z.flag_to_row + k] = 1

        @pl.when(op != NOPS)
        def _():
            @pl.loop(0, by_op[op])
            def _(b):
                c2 = col_of(bucket[op * z.right_op + b]) - col_base

                @pl.when(c2 < ct)
                def _():
                    flag[z.flag_to_row + c2] = 1

            @pl.loop(0, n_col)
            def _(b):
                @pl.when(op_of(cols_over[b]) == op)
                def _():
                    plan[N_SEND_CORNER] = 1

    @pl.loop(0, n_col)
    def _(b):
        op = op_of(cols_over[b])

        @pl.when(op == NOPS)
        def _():
            @pl.loop(0, rt)
            def _(k):
                flag[z.flag_to_col + k] = 1

        @pl.when(op != NOPS)
        def _():
            @pl.loop(0, n_left)
            def _(a):
                u = llist[a]
                c1 = col_of(u) - row_base

                @pl.when((op_of(u) == op) & (c1 < rt))
                def _():
                    flag[z.flag_to_col + c1] = 1

    for count, at_list, at_flag, length in (
        (N_SEND_ROW, z.at_send_row, z.flag_to_row, ct),
        (N_SEND_COL, z.at_send_col, z.flag_to_col, rt),
        (N_TAKE_ROW, z.at_take_row, z.flag_need + z.halo_row, ct),
        (N_TAKE_COL, z.at_take_col, z.flag_need + z.halo_col, rt),
    ):

        @pl.loop(0, length)
        def _(k):
            @pl.when(flag[at_flag + k] == 1)
            def _():
                push(count, at_list, k)

    plan[N_TAKE_CORNER] = flag[z.flag_need + z.corner]


def make_plan(z, here, meta):
    return pl.pallas_call(
        functools.partial(plan_kernel, z),
        out_shape=jax.ShapeDtypeStruct((z.plan_size,), jnp.int32),
        in_specs=[SMEM, SMEM],
        out_specs=SMEM,
        scratch_shapes=[
            pltpu.SMEM((z.total,), jnp.int32),
            pltpu.SMEM((z.total,), jnp.int32),
            pltpu.SMEM((z.total,), jnp.int32),
            pltpu.SMEM((z.total,), jnp.int32),
            pltpu.SMEM((z.flag_size,), jnp.int32),
            pltpu.SMEM((NOPS + 1,), jnp.int32),
            pltpu.SMEM(((NOPS + 1) * z.right_op,), jnp.int32),
        ],
        cost_estimate=pl.CostEstimate(
            flops=0, bytes_accessed=20_000_000, transcendentals=0
        ),
        name="plan",
    )(here, meta)


def block_at(z, ref, block):
    r, c = block // z.ct, block % z.ct
    return ref.at[
        :,
        pl.ds(pl.multiple_of(r * z.edge, z.edge), z.edge),
        pl.ds(pl.multiple_of(c * z.edge, z.edge), z.edge),
    ]


def start_block(z, plan, base, changed, block, target, sem):
    if changed is None:
        pltpu.make_async_copy(block_at(z, base, block), target, sem).start()
        return
    written = plan[z.at_hit + block] != 0

    @pl.when(written)
    def _():
        pltpu.make_async_copy(block_at(z, changed, block), target, sem).start()

    @pl.when(jnp.logical_not(written))
    def _():
        pltpu.make_async_copy(block_at(z, base, block), target, sem).start()


def pack(z, plan, base, changed, first, row_n, col_n):
    row_lo = 0 if first else z.row_slots
    col_lo = 0 if first else z.col_slots
    lengths = [row_n, max(col_n, 1)] + ([1] if first else [])

    def kernel(plan, *refs):
        base_ref = refs[0]
        changed_ref = refs[1] if changed is not None else None
        outs = refs[-1 - len(lengths) : -1]
        sem = refs[-1]
        n_row = jnp.clip(plan[N_SEND_ROW] - row_lo, 0, row_n)
        n_col = jnp.clip(plan[N_SEND_COL] - col_lo, 0, col_n)
        n_all = n_row + n_col

        @pl.loop(0, n_row)
        def _(k):
            block = plan[z.at_send_row + row_lo + k]
            start_block(z, plan, base_ref, changed_ref, block, outs[0].at[k], sem)

        @pl.loop(0, n_col)
        def _(k):
            block = plan[z.at_send_col + col_lo + k] * z.ct
            start_block(z, plan, base_ref, changed_ref, block, outs[1].at[k], sem)

        if first:
            n_all = n_all + plan[N_SEND_CORNER]

            @pl.when(plan[N_SEND_CORNER] == 1)
            def _():
                start_block(z, plan, base_ref, changed_ref, 0, outs[2].at[0], sem)

        @pl.loop(0, n_all)
        def _(k):
            pltpu.make_async_copy(block_at(z, base_ref, 0), outs[0].at[0], sem).wait()

    operands = [plan, base] + ([changed] if changed is not None else [])
    block = (2, z.edge, z.edge)
    return pl.pallas_call(
        kernel,
        out_shape=[jax.ShapeDtypeStruct((n,) + block, jnp.float32) for n in lengths],
        in_specs=[SMEM] + [ANY] * (len(operands) - 1),
        out_specs=[pl.BlockSpec(memory_space=pltpu.VMEM)] * len(lengths),
        scratch_shapes=[pltpu.SemaphoreType.DMA],
        name="pack",
    )(*operands)


def exchange(z, plan, kind, base, changed, packed):
    n, m = z.row_total, z.col_total
    row_route = [(i + 1, i) for i in range(n - 1)]
    col_route = [(j + 1, j) for j in range(m - 1)]
    both_route = [
        ((i + 1) * m + j + 1, i * m + j) for i in range(n - 1) for j in range(m - 1)
    ]
    row_buf, col_buf, corner_buf = packed
    row_in = lax.ppermute(row_buf, "row", row_route)
    col_in = lax.ppermute(col_buf, "col", col_route)
    corner_in = lax.ppermute(corner_buf, BOTH, both_route)
    sizes = extra_sizes(z)
    full = (sizes[-1][0], max(sizes[-1][1], 1))
    if full[0] == 0:
        return row_in, col_in, corner_in

    def run(row_n, col_n):
        def branch(plan, base, changed):
            row_buf, col_buf = pack(z, plan, base, changed, False, row_n, col_n)
            moved = (
                lax.ppermute(row_buf, "row", row_route),
                lax.ppermute(col_buf, "col", col_route),
            )
            return tuple(
                jnp.pad(x, ((0, n - x.shape[0]), (0, 0), (0, 0), (0, 0)))
                for x, n in zip(moved, full)
            )

        return branch

    def skip(plan, base, changed):
        def kernel(plan, *outs):
            pass

        block = (2, z.edge, z.edge)
        return tuple(
            pl.pallas_call(
                kernel,
                out_shape=[jax.ShapeDtypeStruct((n,) + block, jnp.float32) for n in full],
                in_specs=[SMEM],
                out_specs=[ANY, ANY],
                name="skip",
            )(plan)
        )

    branches = [skip] + [run(*size) for size in sizes]
    rest = lax.switch(kind, branches, plan, base, changed)
    return row_in, col_in, corner_in, *rest


def extra_kind(z, rows, cols, ops):
    jump = ops < NOPS
    same = (ops[:, None] == ops[None, :]) & jump[:, None]
    places = jnp.arange(z.row_total * z.rt)

    def most(edge, other, full):
        slab = rows // edge
        over = (cols != rows) & (cols % edge == 0)
        own = slab[:, None] == jnp.arange(places.shape[0] // edge)[None, :]
        picked = over[:, None] & own
        hit = jnp.any(picked[:, None, :] & same[:, :, None], axis=0)
        inside = rows // other == cols // other
        at = (cols[:, None] == places[None, :]) & inside[:, None]
        read = jnp.any(hit[:, :, None] & at[:, None, :], axis=0)
        counts = jnp.sum(
            read.reshape(read.shape[0], -1, other), axis=2, dtype=jnp.int32
        )
        whole = jnp.any(over & (ops == NOPS))
        return jnp.maximum(jnp.max(counts), jnp.where(whole, full, 0))

    row_most = most(z.rt, z.ct, z.ct)
    col_most = most(z.ct, z.rt, z.rt)
    kind = jnp.int32(0)
    for row_slots, col_slots in [(0, 0)] + extra_sizes(z)[:-1]:
        short = (row_most > z.row_slots + row_slots) | (
            col_most > z.col_slots + col_slots
        )
        kind = kind + short.astype(jnp.int32)
    return kind


def extra_sizes(z):
    sizes = [
        (min(z.row_slots, z.ct - z.row_slots), min(z.col_slots, z.rt - z.col_slots)),
        (z.ct - z.row_slots, z.rt - z.col_slots),
    ]
    return sizes[:1] if sizes[0] == sizes[1] else sizes


def halves(x):
    high = x.astype(jnp.bfloat16)
    return high, (x - high.astype(jnp.float32)).astype(jnp.bfloat16)


def dot(a, b):
    return jnp.dot(a, b, preferred_element_type=jnp.float32)


def wait_each(count, copy):
    @pl.loop(0, count)
    def _(k):
        copy.wait()


def load_halo(z, plan, halo, cur, shift, sem):
    row_in, col_in, corner_in = halo[:3]
    for count, at_list, start, slots, first, second in (
        (N_TAKE_ROW, z.at_take_row, z.halo_row, z.row_slots, row_in, halo[3:4]),
        (N_TAKE_COL, z.at_take_col, z.halo_col, z.col_slots, col_in, halo[4:5]),
    ):
        n = plan[count]

        @pl.loop(0, jnp.minimum(n, slots))
        def _(k):
            place = cur.at[start + plan[at_list + k] - shift]
            pltpu.make_async_copy(first.at[k], place, sem).start()

        if second:

            @pl.loop(slots, n)
            def _(k):
                place = cur.at[start + plan[at_list + k] - shift]
                pltpu.make_async_copy(second[0].at[k - slots], place, sem).start()

    @pl.when(plan[N_TAKE_CORNER] == 1)
    def _():
        pltpu.make_async_copy(corner_in.at[0], cur.at[z.corner - shift], sem).start()

    return plan[N_TAKE_ROW] + plan[N_TAKE_COL] + plan[N_TAKE_CORNER]


class Work:
    def __init__(self, z, gain, plan, cur, acc, shift):
        self.z, self.gain, self.plan = z, gain, plan
        self.cur, self.acc, self.shift = cur, acc, shift

    def scaled(self, part):
        return part if self.gain == 1 else self.gain * part

    def left_times(self, tile, block):
        edge = self.z.edge
        high, low = halves(self.cur[block - self.shift].reshape(2 * edge, edge))
        both = dot(tile[0], jnp.concatenate([high, low], axis=1))
        return both[:, :edge] + (both[:, edge:] + dot(tile[1], high))

    def times_right(self, y, tile):
        rows = y.shape[0]
        high, low = halves(y)
        both = dot(jnp.concatenate([high, low], axis=0), tile[0])
        return both[:rows] + (both[rows:] + dot(high, tile[1]))

    def flat(self, block):
        value = self.cur[block - self.shift]
        return jnp.concatenate([value[0], value[1]], axis=1)

    def add_wide(self, block, part):
        edge = self.z.edge
        part = self.scaled(part)
        self.acc[block, 0] += part[:, :edge]
        self.acc[block, 1] += part[:, edge:]

    def ham_left(self, q, tile):
        z, edge = self.z, self.z.edge
        dst = self.plan[z.at_kl_dst + q]
        src = self.plan[z.at_kl_src + q]

        @pl.loop(0, z.ct // UNROLL)
        def _(g):
            cols = [g * UNROLL + u for u in range(UNROLL)]
            parts = []
            for a, b in zip(cols[::2], cols[1::2]):
                x = [
                    self.cur[src + c - self.shift].reshape(2 * edge, edge) for c in (a, b)
                ]
                high, low = halves(jnp.concatenate(x, axis=1))
                part = dot(tile[0], high) + (dot(tile[0], low) + dot(tile[1], high))
                parts += [part[:, :edge], part[:, edge:]]
            for c, part in zip(cols, parts):
                self.acc[dst + c] += self.scaled(part.reshape(2, edge, edge))

    def ham_right(self, q, tile, far):
        z, edge = self.z, self.z.edge
        dst = self.plan[z.at_kr_dst + q]
        src = self.plan[z.at_kr_src + q]

        @pl.loop(0, z.rt // UNROLL)
        def _(g):
            rows = [g * UNROLL + u for u in range(UNROLL)]
            y = jnp.concatenate(
                [self.flat(src + (r if far else r * z.ct)) for r in rows], axis=0
            )
            parts = self.times_right(y, tile)
            for u, r in enumerate(rows):
                self.add_wide(r * z.ct + dst, parts[u * edge : (u + 1) * edge])

    def pairs(self, side, g, left_of, right_of):
        z, plan, edge = self.z, self.plan, self.z.edge
        spots = [g * UNROLL + u for u in range(UNROLL)]
        at_src = getattr(z, "at_" + side + "_src")
        at_dst = getattr(z, "at_" + side + "_dst")
        firsts = [
            self.left_times(left_of(u, p), plan[at_src + p]) for u, p in enumerate(spots)
        ]
        parts = [
            self.times_right(
                jnp.concatenate([first[:edge], first[edge:]], axis=1), right_of(u, p)
            )
            for (u, p), first in zip(enumerate(spots), firsts)
        ]
        for p, part in zip(spots, parts):
            self.add_wide(plan[at_dst + p], part)


def store_blocks(z, plan, count, at_list, acc, out, sem):
    n = plan[count]

    @pl.loop(0, n)
    def _(k):
        block = plan[at_list + k]
        pltpu.make_async_copy(acc.at[block], block_at(z, out, block), sem).start()

    wait_each(n, pltpu.make_async_copy(acc.at[0], block_at(z, out, 0), sem))


def load_blocks(z, plan, count, at_list, src, acc, sem):
    @pl.loop(0, plan[count])
    def _(k):
        block = plan[at_list + k]
        pltpu.make_async_copy(block_at(z, src, block), acc.at[block], sem).start()


def groups(n):
    return (n + UNROLL - 1) // UNROLL


def tile_shape(z, count):
    return (count, 2, 2 * z.edge, 2 * z.edge)


SCALE = 0.5 * TIME_STEP


def stage_kernel(z, second, plan, *refs):
    if second:
        lefts_in, rights_in, base, changed, _, out = refs[:6]
        refs = refs[6:]
        halo = None
    else:
        tiles, base = refs[: z.arrays], refs[z.arrays]
        halo = refs[z.arrays + 1 : -12]
        out, lefts_out, rights_out = refs[-11:-8]
        changed = None
        refs = refs[-8:]
    cur, acc, lefts, rights, ring, ring_sem, sems, tile_sem = refs
    cur_sem, acc_sem, out_sem = (sems.at[k] for k in range(3))
    edge = z.edge
    n_left, n_right = plan[N_LEFT], plan[N_RIGHT]
    n_kl, n_kr = plan[N_KL], plan[N_KR]
    n_tiles = n_left + n_right + n_kl + n_kr
    kept = (
        (n_kl, z.left_max, lefts, 0),
        (n_kr, z.right_max, rights, 1),
        (n_left, 0, lefts, 0),
        (n_right, 0, rights, 1),
    )

    if second:
        for count, start, place, which in kept:
            source = (lefts_in, rights_in)[which]

            @pl.loop(0, count)
            def _(k):
                pltpu.make_async_copy(
                    source.at[start + k], place.at[start + k], tile_sem
                ).start()

    n_read = plan[N_READ]

    @pl.loop(0, n_read)
    def _(k):
        block = plan[z.at_read + k]
        start_block(z, plan, base, changed, block, cur.at[block], cur_sem)

    hits = (N_HIT_OWN, z.at_hit_own) if second else (N_HIT_ALL, z.at_hit_all)
    load_blocks(z, plan, *hits, base, acc, acc_sem)

    if second:
        wait_each(
            n_tiles, pltpu.make_async_copy(lefts_in.at[0], lefts.at[0], tile_sem)
        )
    else:
        n_read = n_read + load_halo(z, plan, halo, cur, 0, cur_sem)

        def prepare(count, at_tile, start, place, target, build):
            def fetch(k):
                s = k % RING
                tile = plan[at_tile + k]
                array, at = tile // PLACES, tile % PLACES
                for which, source in enumerate(tiles):

                    @pl.when(array == which)
                    def _():
                        pltpu.make_async_copy(
                            source.at[at], ring.at[s], ring_sem.at[s]
                        ).start()

            @pl.loop(0, jnp.minimum(count, RING))
            def _(k):
                fetch(k)

            @pl.loop(0, count)
            def _(k):
                s = k % RING
                pltpu.make_async_copy(tiles[0].at[0], ring.at[s], ring_sem.at[s]).wait()
                quads = build(ring[k % RING, 0], ring[k % RING, 1])
                for part in (0, 1):
                    for row in (0, 1):
                        for col in (0, 1):
                            place[
                                start + k,
                                part,
                                row * edge : (row + 1) * edge,
                                col * edge : (col + 1) * edge,
                            ] = quads[row][col][part]
                pltpu.make_async_copy(
                    place.at[start + k], target.at[start + k], tile_sem
                ).start()

                @pl.when(k + RING < count)
                def _():
                    fetch(k + RING)

        def plain(re, im):
            minus = tuple(-part for part in im)
            return ((re, minus), (im, re))

        def turned(re, im):
            minus = tuple(-part for part in re)
            return ((im, re), (minus, im))

        def build_left(re, im):
            return plain(halves(re), halves(im))

        def build_right(re, im):
            return plain(halves((re * SCALE).T), halves((im * SCALE).T))

        def build_kr(re, im):
            return turned(halves((re * SCALE).T), halves((im * SCALE).T))

        def build_kl(re, im):
            return turned(halves(re * SCALE), halves(im * SCALE))

        prepare(n_kl, z.at_kl_tile, z.left_max, lefts, lefts_out, build_kl)
        prepare(n_kr, z.at_kr_tile, z.right_max, rights, rights_out, build_kr)
        prepare(n_left, z.at_left_tile, 0, lefts, lefts_out, build_left)
        prepare(n_right, z.at_right_tile, 0, rights, rights_out, build_right)

    wait_each(n_read, pltpu.make_async_copy(block_at(z, base, 0), cur.at[0], cur_sem))
    wait_each(
        plan[hits[0]], pltpu.make_async_copy(block_at(z, base, 0), acc.at[0], acc_sem)
    )
    work = Work(z, 2 if second else 1, plan, cur, acc, 0)

    def tile_of(store, slot):
        return store[slot, 0], store[slot, 1]

    @pl.loop(0, n_kl)
    def _(q):
        far = plan[z.at_kl_src + q] >= z.blocks

        @pl.when(jnp.logical_not(far) if second else True)
        def _():
            work.ham_left(q, tile_of(lefts, z.left_max + q))

    @pl.loop(0, n_kr)
    def _(q):
        far = plan[z.at_kr_src + q] >= z.blocks
        tile = tile_of(rights, z.right_max + q)

        @pl.when(jnp.logical_not(far))
        def _():
            work.ham_right(q, tile, False)

        if not second:

            @pl.when(far)
            def _():
                work.ham_right(q, tile, True)

    for count, side in ((N_OWN, "own"), (N_FAR, "far"))[: 1 if second else 2]:
        at_left = getattr(z, "at_" + side + "_left")
        at_right = getattr(z, "at_" + side + "_right")

        @pl.loop(0, groups(plan[count]))
        def _(g):
            work.pairs(
                side,
                g,
                lambda u, p: tile_of(lefts, plan[at_left + p]),
                lambda u, p: tile_of(rights, plan[at_right + p]),
            )

    store_blocks(z, plan, *hits, acc, out, out_sem)
    if not second:
        wait_each(
            n_tiles, pltpu.make_async_copy(lefts.at[0], lefts_out.at[0], tile_sem)
        )


def far_kernel(z, n_halo, plan, lefts_in, rights_in, result, *refs):
    halo = refs[:n_halo]
    out, cur, acc, lefts, rights, sems = refs[n_halo:]
    cur_sem, acc_sem, out_sem, tile_sem = (sems.at[k] for k in range(4))
    n_read = load_halo(z, plan, halo, cur, z.blocks, cur_sem)
    load_blocks(z, plan, N_HIT_FAR, z.at_hit_far, result, acc, acc_sem)
    wait_each(n_read, pltpu.make_async_copy(halo[2].at[0], cur.at[0], cur_sem))
    wait_each(
        plan[N_HIT_FAR],
        pltpu.make_async_copy(block_at(z, result, 0), acc.at[0], acc_sem),
    )
    work = Work(z, 2, plan, cur, acc, z.blocks)

    def bring(slot, source, place):
        copy = pltpu.make_async_copy(source.at[slot], place, tile_sem)
        copy.start()
        return copy

    @pl.loop(0, groups(plan[N_FAR]))
    def _(g):
        copies = []
        for u in range(UNROLL):
            p = g * UNROLL + u
            copies.append(bring(plan[z.at_far_left + p], lefts_in, lefts.at[u]))
            copies.append(bring(plan[z.at_far_right + p], rights_in, rights.at[u]))
        for copy in copies:
            copy.wait()
        work.pairs(
            "far",
            g,
            lambda u, p: (lefts[u, 0], lefts[u, 1]),
            lambda u, p: (rights[u, 0], rights[u, 1]),
        )

    @pl.loop(0, plan[N_KL])
    def _(q):
        @pl.when(plan[z.at_kl_src + q] >= z.blocks)
        def _():
            bring(z.left_max + q, lefts_in, lefts.at[0]).wait()
            work.ham_left(q, (lefts[0, 0], lefts[0, 1]))

    @pl.loop(0, plan[N_KR])
    def _(q):
        @pl.when(plan[z.at_kr_src + q] >= z.blocks)
        def _():
            bring(z.right_max + q, rights_in, rights.at[0]).wait()
            work.ham_right(q, (rights[0, 0], rights[0, 1]), True)

    store_blocks(z, plan, N_HIT_FAR, z.at_hit_far, acc, out, out_sem)


PARAMS = pltpu.CompilerParams(vmem_limit_bytes=58 * 1024 * 1024)


def copy_of(z, base):
    spec = pl.BlockSpec((2, z.edge, base.shape[2]), lambda r: (0, r, 0))

    def kernel(src, dst):
        dst[...] = src[...]

    return pl.pallas_call(
        kernel,
        out_shape=jax.ShapeDtypeStruct(base.shape, jnp.float32),
        grid=(z.rt,),
        in_specs=[spec],
        out_specs=spec,
        cost_estimate=pl.CostEstimate(
            flops=0, bytes_accessed=2 * base.size * 4, transcendentals=0
        ),
        name="copy_of",
    )(base)


def first_stage(z, plan, tiles, base, halo, result):
    block = (2, z.edge, z.edge)
    lefts = tile_shape(z, z.left_max + CAP)
    rights = tile_shape(z, z.right_max + z.right_op)
    return pl.pallas_call(
        functools.partial(stage_kernel, z, False),
        out_shape=[
            jax.ShapeDtypeStruct(base.shape, jnp.float32),
            jax.ShapeDtypeStruct(lefts, jnp.bfloat16),
            jax.ShapeDtypeStruct(rights, jnp.bfloat16),
        ],
        in_specs=[SMEM] + [ANY] * (2 + len(tiles) + len(halo)),
        out_specs=[ANY] * 3,
        scratch_shapes=[
            pltpu.VMEM((z.corner + 1,) + block, jnp.float32),
            pltpu.VMEM((z.blocks + 1,) + block, jnp.float32),
            pltpu.VMEM(lefts, jnp.bfloat16),
            pltpu.VMEM(rights, jnp.bfloat16),
            pltpu.VMEM((RING,) + block, jnp.float32),
            pltpu.SemaphoreType.DMA((RING,)),
            pltpu.SemaphoreType.DMA((3,)),
            pltpu.SemaphoreType.DMA,
        ],
        compiler_params=PARAMS,
        cost_estimate=COST,
        name="stage_one",
    )(plan, *tiles, base, *halo, result)


COST = pl.CostEstimate(flops=4_000_000_000, bytes_accessed=48_000_000, transcendentals=0)


def second_stage(z, plan, lefts, rights, base, middle, result):
    block = (2, z.edge, z.edge)
    return pl.pallas_call(
        functools.partial(stage_kernel, z, True),
        out_shape=jax.ShapeDtypeStruct(base.shape, jnp.float32),
        in_specs=[SMEM] + [ANY] * 5,
        out_specs=ANY,
        scratch_shapes=[
            pltpu.VMEM((z.blocks,) + block, jnp.float32),
            pltpu.VMEM((z.blocks + 1,) + block, jnp.float32),
            pltpu.VMEM(lefts.shape, jnp.bfloat16),
            pltpu.VMEM(rights.shape, jnp.bfloat16),
            pltpu.VMEM((1,) + block, jnp.float32),
            pltpu.SemaphoreType.DMA((1,)),
            pltpu.SemaphoreType.DMA((3,)),
            pltpu.SemaphoreType.DMA,
        ],
        input_output_aliases={5: 0},
        compiler_params=PARAMS,
        cost_estimate=COST,
        name="stage_two",
    )(plan, lefts, rights, base, middle, result)


def far_stage(z, plan, lefts, rights, result, halo):
    block = (2, z.edge, z.edge)
    return pl.pallas_call(
        functools.partial(far_kernel, z, len(halo)),
        out_shape=jax.ShapeDtypeStruct(result.shape, jnp.float32),
        in_specs=[SMEM] + [ANY] * (3 + len(halo)),
        out_specs=ANY,
        scratch_shapes=[
            pltpu.VMEM((z.corner + 1 - z.blocks,) + block, jnp.float32),
            pltpu.VMEM((z.blocks + 1,) + block, jnp.float32),
            pltpu.VMEM(tile_shape(z, UNROLL), jnp.bfloat16),
            pltpu.VMEM(tile_shape(z, UNROLL), jnp.bfloat16),
            pltpu.SemaphoreType.DMA((4,)),
        ],
        input_output_aliases={3: 0},
        compiler_params=PARAMS,
        name="far",
    )(plan, lefts, rights, result, *halo)


def swapped(value, row_mask, col_mask):
    n, m = lax.axis_size("row"), lax.axis_size("col")
    if not col_mask:
        return lax.ppermute(value, "row", [(i, i ^ row_mask) for i in range(n)])
    if not row_mask:
        return lax.ppermute(value, "col", [(j, j ^ col_mask) for j in range(m)])
    route = [
        (i * m + j, (i ^ row_mask) * m + (j ^ col_mask)) for i in range(n) for j in range(m)
    ]
    return lax.ppermute(value, BOTH, route)


def near_tiles(own):
    return [swapped(own, *mask) for mask in ((4, 0), (2, 0), (0, 2), (1, 0), (1, 2))]


def gather_tiles(own, near, settle):
    z4, z2, x, y, d = near
    line = jnp.concatenate([z2, z4], axis=0)
    first = jnp.concatenate([own, line, x, y, d], axis=0)
    z6 = swapped(z4, 2, 0)
    x_line = swapped(line, 0, 2)
    y_line = swapped(line, 1, 0)
    d4 = swapped(d, 4, 0)
    d2 = swapped(d, 2, 0)
    (z6, x_line, y_line, d4, d2, first), kept = settle((z6, x_line, y_line, d4, d2, first))
    last = [swapped(z6, 0, 2), swapped(z6, 1, 0), swapped(d4, 2, 0)]
    first_other = swapped(first, 0, 1)
    second = jnp.concatenate([z6, x_line, y_line, d4, d2], axis=0)
    second_other = swapped(second, 0, 1)
    third = jnp.concatenate(last, axis=0)
    third_other = swapped(third, 0, 1)
    return [first, second, third, first_other, second_other, third_other], kept


HOPS = (
    (0, 0), (0, 4), (0, 3), (0, 5),
    (0, 1), (1, 3), (1, 1), (1, 6),
    (0, 2), (1, 4), (1, 2), (1, 5),
    (1, 0), (2, 1), (2, 0), (2, 2),
)


def local(state, tile_vals, tile_row, tile_col, tile_op):
    z = Sizes(state, tile_vals)
    meta = jnp.stack([tile_row, tile_col, tile_op])
    spread = jnp.broadcast_to(meta[None], (z.row_total * z.col_total,) + meta.shape)
    gathered = lax.all_to_all(spread, BOTH, 0, 0, tiled=True)
    if z.by_hops:
        near = near_tiles(tile_vals)
    else:
        tiles = [lax.all_gather(tile_vals, BOTH, axis=0, tiled=True)]
    meta = jnp.swapaxes(gathered, 0, 1).reshape(3, z.total)
    table = [jnp.int32(array * PLACES + at) for array, at in HOPS]
    here = jnp.stack(
        [lax.axis_index("row").astype(jnp.int32), lax.axis_index("col").astype(jnp.int32)]
        + table
    )
    plan = make_plan(z, here, meta.reshape(-1))
    kind = extra_kind(z, meta[0], meta[1], meta[2])
    packed = pack(z, plan, state, None, True, z.row_slots, z.col_slots)
    if z.by_hops:
        near, plan, packed = lax.optimization_barrier((near, plan, packed))
    halo = exchange(z, plan, kind, state, None, packed)
    result = copy_of(z, state)
    if z.by_hops:

        def settle(values):
            return lax.optimization_barrier((values, (halo, result)))

        tiles, (halo, result) = gather_tiles(tile_vals, near, settle)
    middle, lefts, rights = first_stage(z, plan, tiles, state, halo, result)
    packed = pack(z, plan, state, middle, True, z.row_slots, z.col_slots)
    halo = exchange(z, plan, kind, state, middle, packed)
    result = second_stage(z, plan, lefts, rights, state, middle, result)
    return far_stage(z, plan, lefts, rights, result, halo)


def solution(mesh):
    placed = (
        P(None, "row", "col"),
        P(("row", "col"), None, None, None),
        P(("row", "col")),
        P(("row", "col")),
        P(("row", "col")),
    )
    return jax.shard_map(
        local, mesh=mesh, in_specs=placed, out_specs=P(None, "row", "col"), check_vma=False
    )
```

```python
import functools

import jax
import jax.numpy as jnp
from jax import lax
from jax.experimental import pallas as pl
from jax.experimental.pallas import tpu as pltpu
from jax.sharding import PartitionSpec as P

NOPS = 16
CAP = 2
TIME_STEP = 0.25
UNROLL = 4
RING = 8
SLOTS = 4
PLACES = 1024
BOTH = ("row", "col")
ANY = pl.BlockSpec(memory_space=pl.ANY)
SMEM = pl.BlockSpec(memory_space=pltpu.SMEM)


class Sizes:
    def __init__(self, state, tile_vals):
        self.row_total = lax.axis_size("row")
        self.col_total = lax.axis_size("col")
        self.edge = tile_vals.shape[-1]
        self.own = tile_vals.shape[0]
        self.total = self.own * self.row_total * self.col_total
        self.rt = state.shape[1] // self.edge
        self.ct = state.shape[2] // self.edge
        self.span = self.ct // self.rt
        self.left_max = CAP * self.row_total
        self.right_max = self.span * self.left_max
        self.right_op = self.span * CAP
        self.pair_max = self.left_max * self.right_op
        self.pair_pad = -(-self.pair_max // UNROLL) * UNROLL
        self.blocks = self.rt * self.ct
        self.halo_row = self.blocks
        self.halo_col = self.blocks + self.ct
        self.corner = self.blocks + self.ct + self.rt
        self.row_slots = min(SLOTS, self.ct)
        self.col_slots = min(SLOTS, self.rt)
        place = 0
        for name, length in (
            ("counts", 16),
            ("left_tile", self.left_max),
            ("right_tile", self.right_max),
            ("kl_tile", CAP),
            ("kl_dst", CAP),
            ("kl_src", CAP),
            ("kr_tile", self.right_op),
            ("kr_dst", self.right_op),
            ("kr_src", self.right_op),
            ("own_left", self.pair_pad),
            ("own_right", self.pair_pad),
            ("own_src", self.pair_pad),
            ("own_dst", self.pair_pad),
            ("far_left", self.pair_pad),
            ("far_right", self.pair_pad),
            ("far_src", self.pair_pad),
            ("far_dst", self.pair_pad),
            ("read", self.blocks),
            ("hit_own", self.blocks),
            ("hit_far", self.blocks),
            ("hit_all", self.blocks),
            ("hit", self.blocks),
            ("send_row", self.ct),
            ("send_col", self.rt),
            ("take_row", self.ct),
            ("take_col", self.rt),
        ):
            setattr(self, "at_" + name, place)
            place += length
        self.plan_size = -(-place // 128) * 128
        self.by_hops = (self.row_total, self.col_total) == (8, 4)
        self.arrays = 6 if self.by_hops else 1
        place = 0
        for name, length in (
            ("need", self.corner + 1),
            ("to_row", self.ct),
            ("to_col", self.rt),
        ):
            setattr(self, "flag_" + name, place)
            place += length
        self.flag_size = place


    def tile_place(self, tile, here):
        if not self.by_hops:
            return tile
        device = tile // self.own
        row = (device // self.col_total) ^ here[0]
        col = (device % self.col_total) ^ here[1]
        hop = here[2 + ((row // 2) * 4 + ((row & 1) | (col & 2)))]
        array = hop // PLACES + (col & 1) * 3
        return array * PLACES + (hop % PLACES) * self.own + tile % self.own


(
    N_LEFT,
    N_RIGHT,
    N_KL,
    N_KR,
    N_OWN,
    N_FAR,
    N_READ,
    N_HIT_OWN,
    N_HIT_FAR,
    N_HIT_ALL,
    N_SEND_ROW,
    N_SEND_COL,
    N_SEND_CORNER,
    N_TAKE_ROW,
    N_TAKE_COL,
    N_TAKE_CORNER,
) = range(16)
OWN, FAR = 1, 2


def plan_kernel(z, here, meta, plan, llist, rows_over, cols_over, slot, flag, by_op, bucket):
    me_row, me_col = here[0], here[1]
    rt, ct = z.rt, z.ct
    row_base = me_row * rt
    col_base = me_col * ct

    def row_of(t):
        return meta[t]

    def col_of(t):
        return meta[z.total + t]

    def op_of(t):
        return meta[2 * z.total + t]

    def clear(ref, start, length):
        step = 8

        @pl.loop(0, length // step)
        def _(k):
            for u in range(step):
                ref[start + k * step + u] = 0

        for k in range(length // step * step, length):
            ref[start + k] = 0

    clear(plan, 0, 16)
    clear(plan, z.at_hit, z.blocks)
    clear(flag, 0, z.flag_size)
    clear(by_op, 0, NOPS + 1)

    def place(tile):
        return z.tile_place(tile, here)

    def push(counter, at_list, value):
        k = plan[counter]
        plan[at_list + k] = value
        plan[counter] = k + 1

    def read(block):
        @pl.when(flag[z.flag_need + block] == 0)
        def _():
            flag[z.flag_need + block] = 1

            @pl.when(block < z.blocks)
            def _():
                push(N_READ, z.at_read, block)

    def write(block, kind):
        old = plan[z.at_hit + block]

        @pl.when((old & kind) == 0)
        def _():
            plan[z.at_hit + block] = old | kind

            @pl.when(old == 0)
            def _():
                push(N_HIT_ALL, z.at_hit_all, block)

            @pl.when(kind == OWN)
            def _():
                push(N_HIT_OWN, z.at_hit_own, block)

            @pl.when(kind == FAR)
            def _():
                push(N_HIT_FAR, z.at_hit_far, block)

    def block_id(r, c):
        inside = jnp.where(c < ct, r * ct + c, z.halo_col + r)
        outside = jnp.where(c < ct, z.halo_row + c, z.corner)
        return jnp.where(r < rt, inside, outside)

    def gather(t, found):
        n_left, n_row, n_col = found
        r, c = row_of(t), col_of(t)
        is_left = (r >= row_base) & (r < row_base + rt)
        over_row = (r == row_base - 1) & (c == row_base)
        over_col = (r == col_base - 1) & (c == col_base)

        @pl.when(is_left)
        def _():
            llist[n_left] = t

        @pl.when((r >= col_base) & (r < col_base + ct))
        def _():
            op = op_of(t)
            k = by_op[op]
            bucket[op * z.right_op + k] = t
            by_op[op] = k + 1
            slot[t] = -1

        @pl.when(over_row)
        def _():
            rows_over[n_row] = t

        @pl.when(over_col)
        def _():
            cols_over[n_col] = t

        return (
            n_left + is_left.astype(jnp.int32),
            n_row + over_row.astype(jnp.int32),
            n_col + over_col.astype(jnp.int32),
        )

    n_left, n_row, n_col = lax.fori_loop(0, z.total, gather, (jnp.int32(0),) * 3)

    def one_left(a, _):
        t = llist[a]
        op = op_of(t)
        r1 = row_of(t) - row_base
        c1 = col_of(t) - row_base

        @pl.when(op == NOPS)
        def _():
            k = plan[N_KL]
            plan[z.at_kl_tile + k] = place(t)
            plan[z.at_kl_dst + k] = r1 * ct
            plan[z.at_kl_src + k] = c1 * ct
            plan[N_KL] = k + 1
            kind = jnp.where(c1 < rt, OWN, FAR)

            @pl.loop(0, ct)
            def _(c):
                read(c1 * ct + c)
                write(r1 * ct + c, kind)

        @pl.when(op != NOPS)
        def _():
            mine = plan[N_LEFT]
            n_match = by_op[op]

            @pl.loop(0, n_match)
            def _(b):
                u = bucket[op * z.right_op + b]

                @pl.when(slot[u] < 0)
                def _():
                    slot[u] = plan[N_RIGHT]
                    push(N_RIGHT, z.at_right_tile, place(u))

                r2 = row_of(u) - col_base
                c2 = col_of(u) - col_base
                own = (c1 < rt) & (c2 < ct)
                src = block_id(c1, c2)
                dst = r1 * ct + r2

                @pl.when(own)
                def _():
                    k = plan[N_OWN]
                    plan[z.at_own_left + k] = mine
                    plan[z.at_own_right + k] = slot[u]
                    plan[z.at_own_src + k] = src
                    plan[z.at_own_dst + k] = dst
                    plan[N_OWN] = k + 1

                @pl.when(jnp.logical_not(own))
                def _():
                    k = plan[N_FAR]
                    plan[z.at_far_left + k] = mine
                    plan[z.at_far_right + k] = slot[u]
                    plan[z.at_far_src + k] = src
                    plan[z.at_far_dst + k] = dst
                    plan[N_FAR] = k + 1

                read(src)
                write(dst, jnp.where(own, OWN, FAR))

            @pl.when(n_match > 0)
            def _():
                push(N_LEFT, z.at_left_tile, place(t))

        return 0

    lax.fori_loop(0, n_left, one_left, 0)

    @pl.loop(0, by_op[NOPS])
    def _(k):
        u = bucket[NOPS * z.right_op + k]
        r2 = row_of(u) - col_base
        c2 = col_of(u) - col_base
        own = c2 < ct
        plan[z.at_kr_tile + k] = place(u)
        plan[z.at_kr_dst + k] = r2
        plan[z.at_kr_src + k] = jnp.where(own, c2, z.halo_col)
        kind = jnp.where(own, OWN, FAR)

        @pl.loop(0, rt)
        def _(r):
            read(block_id(r, c2))
            write(r * ct + r2, kind)

    plan[N_KR] = by_op[NOPS]

    for count, side, src in ((N_OWN, "own", 0), (N_FAR, "far", z.halo_row)):
        n = plan[count]

        @pl.loop(n, (n + UNROLL - 1) // UNROLL * UNROLL)
        def _(k):
            plan[getattr(z, "at_" + side + "_left") + k] = 0
            plan[getattr(z, "at_" + side + "_right") + k] = 0
            plan[getattr(z, "at_" + side + "_src") + k] = src
            plan[getattr(z, "at_" + side + "_dst") + k] = z.blocks

    @pl.loop(0, n_row)
    def _(a):
        op = op_of(rows_over[a])

        @pl.when(op == NOPS)
        def _():
            @pl.loop(0, ct)
            def _(k):
                flag[z.flag_to_row + k] = 1

        @pl.when(op != NOPS)
        def _():
            @pl.loop(0, by_op[op])
            def _(b):
                c2 = col_of(bucket[op * z.right_op + b]) - col_base

                @pl.when(c2 < ct)
                def _():
                    flag[z.flag_to_row + c2] = 1

            @pl.loop(0, n_col)
            def _(b):
                @pl.when(op_of(cols_over[b]) == op)
                def _():
                    plan[N_SEND_CORNER] = 1

    @pl.loop(0, n_col)
    def _(b):
        op = op_of(cols_over[b])

        @pl.when(op == NOPS)
        def _():
            @pl.loop(0, rt)
            def _(k):
                flag[z.flag_to_col + k] = 1

        @pl.when(op != NOPS)
        def _():
            @pl.loop(0, n_left)
            def _(a):
                u = llist[a]
                c1 = col_of(u) - row_base

                @pl.when((op_of(u) == op) & (c1 < rt))
                def _():
                    flag[z.flag_to_col + c1] = 1

    for count, at_list, at_flag, length in (
        (N_SEND_ROW, z.at_send_row, z.flag_to_row, ct),
        (N_SEND_COL, z.at_send_col, z.flag_to_col, rt),
        (N_TAKE_ROW, z.at_take_row, z.flag_need + z.halo_row, ct),
        (N_TAKE_COL, z.at_take_col, z.flag_need + z.halo_col, rt),
    ):

        @pl.loop(0, length)
        def _(k):
            @pl.when(flag[at_flag + k] == 1)
            def _():
                push(count, at_list, k)

    plan[N_TAKE_CORNER] = flag[z.flag_need + z.corner]


def make_plan(z, here, meta):
    return pl.pallas_call(
        functools.partial(plan_kernel, z),
        out_shape=jax.ShapeDtypeStruct((z.plan_size,), jnp.int32),
        in_specs=[SMEM, SMEM],
        out_specs=SMEM,
        scratch_shapes=[
            pltpu.SMEM((z.total,), jnp.int32),
            pltpu.SMEM((z.total,), jnp.int32),
            pltpu.SMEM((z.total,), jnp.int32),
            pltpu.SMEM((z.total,), jnp.int32),
            pltpu.SMEM((z.flag_size,), jnp.int32),
            pltpu.SMEM((NOPS + 1,), jnp.int32),
            pltpu.SMEM(((NOPS + 1) * z.right_op,), jnp.int32),
        ],
        cost_estimate=pl.CostEstimate(
            flops=0, bytes_accessed=20_000_000, transcendentals=0
        ),
        name="plan",
    )(here, meta)


def block_at(z, ref, block):
    r, c = block // z.ct, block % z.ct
    return ref.at[
        :,
        pl.ds(pl.multiple_of(r * z.edge, z.edge), z.edge),
        pl.ds(pl.multiple_of(c * z.edge, z.edge), z.edge),
    ]


def start_block(z, plan, base, changed, block, target, sem):
    if changed is None:
        pltpu.make_async_copy(block_at(z, base, block), target, sem).start()
        return
    written = plan[z.at_hit + block] != 0

    @pl.when(written)
    def _():
        pltpu.make_async_copy(block_at(z, changed, block), target, sem).start()

    @pl.when(jnp.logical_not(written))
    def _():
        pltpu.make_async_copy(block_at(z, base, block), target, sem).start()


def pack(z, plan, base, changed, first, row_n, col_n):
    row_lo = 0 if first else z.row_slots
    col_lo = 0 if first else z.col_slots
    lengths = [row_n, max(col_n, 1)] + ([1] if first else [])

    def kernel(plan, *refs):
        base_ref = refs[0]
        changed_ref = refs[1] if changed is not None else None
        outs = refs[-1 - len(lengths) : -1]
        sem = refs[-1]
        n_row = jnp.clip(plan[N_SEND_ROW] - row_lo, 0, row_n)
        n_col = jnp.clip(plan[N_SEND_COL] - col_lo, 0, col_n)
        n_all = n_row + n_col

        @pl.loop(0, n_row)
        def _(k):
            block = plan[z.at_send_row + row_lo + k]
            start_block(z, plan, base_ref, changed_ref, block, outs[0].at[k], sem)

        @pl.loop(0, n_col)
        def _(k):
            block = plan[z.at_send_col + col_lo + k] * z.ct
            start_block(z, plan, base_ref, changed_ref, block, outs[1].at[k], sem)

        if first:
            n_all = n_all + plan[N_SEND_CORNER]

            @pl.when(plan[N_SEND_CORNER] == 1)
            def _():
                start_block(z, plan, base_ref, changed_ref, 0, outs[2].at[0], sem)

        @pl.loop(0, n_all)
        def _(k):
            pltpu.make_async_copy(block_at(z, base_ref, 0), outs[0].at[0], sem).wait()

    operands = [plan, base] + ([changed] if changed is not None else [])
    block = (2, z.edge, z.edge)
    return pl.pallas_call(
        kernel,
        out_shape=[jax.ShapeDtypeStruct((n,) + block, jnp.float32) for n in lengths],
        in_specs=[SMEM] + [ANY] * (len(operands) - 1),
        out_specs=[pl.BlockSpec(memory_space=pltpu.VMEM)] * len(lengths),
        scratch_shapes=[pltpu.SemaphoreType.DMA],
        name="pack",
    )(*operands)


def exchange(z, plan, kind, base, changed, packed):
    n, m = z.row_total, z.col_total
    row_route = [(i + 1, i) for i in range(n - 1)]
    col_route = [(j + 1, j) for j in range(m - 1)]
    both_route = [
        ((i + 1) * m + j + 1, i * m + j) for i in range(n - 1) for j in range(m - 1)
    ]
    row_buf, col_buf, corner_buf = packed
    row_in = lax.ppermute(row_buf, "row", row_route)
    col_in = lax.ppermute(col_buf, "col", col_route)
    corner_in = lax.ppermute(corner_buf, BOTH, both_route)
    sizes = extra_sizes(z)
    full = (sizes[-1][0], max(sizes[-1][1], 1))
    if full[0] == 0:
        return row_in, col_in, corner_in

    def run(row_n, col_n):
        def branch(plan, base, changed):
            row_buf, col_buf = pack(z, plan, base, changed, False, row_n, col_n)
            moved = (
                lax.ppermute(row_buf, "row", row_route),
                lax.ppermute(col_buf, "col", col_route),
            )
            return tuple(
                jnp.pad(x, ((0, n - x.shape[0]), (0, 0), (0, 0), (0, 0)))
                for x, n in zip(moved, full)
            )

        return branch

    def skip(plan, base, changed):
        def kernel(plan, *outs):
            pass

        block = (2, z.edge, z.edge)
        return tuple(
            pl.pallas_call(
                kernel,
                out_shape=[jax.ShapeDtypeStruct((n,) + block, jnp.float32) for n in full],
                in_specs=[SMEM],
                out_specs=[ANY, ANY],
                name="skip",
            )(plan)
        )

    branches = [skip] + [run(*size) for size in sizes]
    rest = lax.switch(kind, branches, plan, base, changed)
    return row_in, col_in, corner_in, *rest


def extra_kind(z, rows, cols, ops):
    jump = ops < NOPS
    same = (ops[:, None] == ops[None, :]) & jump[:, None]
    places = jnp.arange(z.row_total * z.rt)

    def most(edge, other, full):
        slab = rows // edge
        over = (cols != rows) & (cols % edge == 0)
        own = slab[:, None] == jnp.arange(places.shape[0] // edge)[None, :]
        picked = over[:, None] & own
        hit = jnp.any(picked[:, None, :] & same[:, :, None], axis=0)
        inside = rows // other == cols // other
        at = (cols[:, None] == places[None, :]) & inside[:, None]
        read = jnp.any(hit[:, :, None] & at[:, None, :], axis=0)
        counts = jnp.sum(
            read.reshape(read.shape[0], -1, other), axis=2, dtype=jnp.int32
        )
        whole = jnp.any(over & (ops == NOPS))
        return jnp.maximum(jnp.max(counts), jnp.where(whole, full, 0))

    row_most = most(z.rt, z.ct, z.ct)
    col_most = most(z.ct, z.rt, z.rt)
    kind = jnp.int32(0)
    for row_slots, col_slots in [(0, 0)] + extra_sizes(z)[:-1]:
        short = (row_most > z.row_slots + row_slots) | (
            col_most > z.col_slots + col_slots
        )
        kind = kind + short.astype(jnp.int32)
    return kind


def extra_sizes(z):
    sizes = [
        (min(z.row_slots, z.ct - z.row_slots), min(z.col_slots, z.rt - z.col_slots)),
        (z.ct - z.row_slots, z.rt - z.col_slots),
    ]
    return sizes[:1] if sizes[0] == sizes[1] else sizes


def halves(x):
    high = x.astype(jnp.bfloat16)
    return high, (x - high.astype(jnp.float32)).astype(jnp.bfloat16)


def dot(a, b):
    return jnp.dot(a, b, preferred_element_type=jnp.float32)


def wait_each(count, copy):
    @pl.loop(0, count)
    def _(k):
        copy.wait()


def load_halo(z, plan, halo, cur, shift, sem):
    row_in, col_in, corner_in = halo[:3]
    for count, at_list, start, slots, first, second in (
        (N_TAKE_ROW, z.at_take_row, z.halo_row, z.row_slots, row_in, halo[3:4]),
        (N_TAKE_COL, z.at_take_col, z.halo_col, z.col_slots, col_in, halo[4:5]),
    ):
        n = plan[count]

        @pl.loop(0, jnp.minimum(n, slots))
        def _(k):
            place = cur.at[start + plan[at_list + k] - shift]
            pltpu.make_async_copy(first.at[k], place, sem).start()

        if second:

            @pl.loop(slots, n)
            def _(k):
                place = cur.at[start + plan[at_list + k] - shift]
                pltpu.make_async_copy(second[0].at[k - slots], place, sem).start()

    @pl.when(plan[N_TAKE_CORNER] == 1)
    def _():
        pltpu.make_async_copy(corner_in.at[0], cur.at[z.corner - shift], sem).start()

    return plan[N_TAKE_ROW] + plan[N_TAKE_COL] + plan[N_TAKE_CORNER]


class Work:
    def __init__(self, z, gain, plan, cur, acc, shift):
        self.z, self.gain, self.plan = z, gain, plan
        self.cur, self.acc, self.shift = cur, acc, shift

    def scaled(self, part):
        return part if self.gain == 1 else self.gain * part

    def left_times(self, tile, block):
        edge = self.z.edge
        high, low = halves(self.cur[block - self.shift].reshape(2 * edge, edge))
        both = dot(tile[0], jnp.concatenate([high, low], axis=1))
        return both[:, :edge] + (both[:, edge:] + dot(tile[1], high))

    def times_right(self, y, tile):
        rows = y.shape[0]
        high, low = halves(y)
        both = dot(jnp.concatenate([high, low], axis=0), tile[0])
        return both[:rows] + (both[rows:] + dot(high, tile[1]))

    def flat(self, block):
        value = self.cur[block - self.shift]
        return jnp.concatenate([value[0], value[1]], axis=1)

    def add_wide(self, block, part):
        edge = self.z.edge
        part = self.scaled(part)
        self.acc[block, 0] += part[:, :edge]
        self.acc[block, 1] += part[:, edge:]

    def ham_left(self, q, tile):
        z, edge = self.z, self.z.edge
        dst = self.plan[z.at_kl_dst + q]
        src = self.plan[z.at_kl_src + q]

        @pl.loop(0, z.ct // UNROLL)
        def _(g):
            cols = [g * UNROLL + u for u in range(UNROLL)]
            parts = []
            for a, b in zip(cols[::2], cols[1::2]):
                x = [
                    self.cur[src + c - self.shift].reshape(2 * edge, edge) for c in (a, b)
                ]
                high, low = halves(jnp.concatenate(x, axis=1))
                part = dot(tile[0], high) + (dot(tile[0], low) + dot(tile[1], high))
                parts += [part[:, :edge], part[:, edge:]]
            for c, part in zip(cols, parts):
                self.acc[dst + c] += self.scaled(part.reshape(2, edge, edge))

    def ham_right(self, q, tile, far):
        z, edge = self.z, self.z.edge
        dst = self.plan[z.at_kr_dst + q]
        src = self.plan[z.at_kr_src + q]

        @pl.loop(0, z.rt // UNROLL)
        def _(g):
            rows = [g * UNROLL + u for u in range(UNROLL)]
            y = jnp.concatenate(
                [self.flat(src + (r if far else r * z.ct)) for r in rows], axis=0
            )
            parts = self.times_right(y, tile)
            for u, r in enumerate(rows):
                self.add_wide(r * z.ct + dst, parts[u * edge : (u + 1) * edge])

    def pairs(self, side, g, left_of, right_of):
        z, plan, edge = self.z, self.plan, self.z.edge
        spots = [g * UNROLL + u for u in range(UNROLL)]
        at_src = getattr(z, "at_" + side + "_src")
        at_dst = getattr(z, "at_" + side + "_dst")
        firsts = [
            self.left_times(left_of(u, p), plan[at_src + p]) for u, p in enumerate(spots)
        ]
        parts = [
            self.times_right(
                jnp.concatenate([first[:edge], first[edge:]], axis=1), right_of(u, p)
            )
            for (u, p), first in zip(enumerate(spots), firsts)
        ]
        for p, part in zip(spots, parts):
            self.add_wide(plan[at_dst + p], part)


def store_blocks(z, plan, count, at_list, acc, out, sem):
    n = plan[count]

    @pl.loop(0, n)
    def _(k):
        block = plan[at_list + k]
        pltpu.make_async_copy(acc.at[block], block_at(z, out, block), sem).start()

    wait_each(n, pltpu.make_async_copy(acc.at[0], block_at(z, out, 0), sem))


def load_blocks(z, plan, count, at_list, src, acc, sem):
    @pl.loop(0, plan[count])
    def _(k):
        block = plan[at_list + k]
        pltpu.make_async_copy(block_at(z, src, block), acc.at[block], sem).start()


def groups(n):
    return (n + UNROLL - 1) // UNROLL


def tile_shape(z, count):
    return (count, 2, 2 * z.edge, 2 * z.edge)


SCALE = 0.5 * TIME_STEP


def stage_kernel(z, second, plan, *refs):
    if second:
        lefts_in, rights_in, base, changed, _, out = refs[:6]
        refs = refs[6:]
        halo = None
    else:
        tiles, base = refs[: z.arrays], refs[z.arrays]
        halo = refs[z.arrays + 1 : -12]
        out, lefts_out, rights_out = refs[-11:-8]
        changed = None
        refs = refs[-8:]
    cur, acc, lefts, rights, ring, ring_sem, sems, tile_sem = refs
    cur_sem, acc_sem, out_sem = (sems.at[k] for k in range(3))
    edge = z.edge
    n_left, n_right = plan[N_LEFT], plan[N_RIGHT]
    n_kl, n_kr = plan[N_KL], plan[N_KR]
    n_tiles = n_left + n_right + n_kl + n_kr
    kept = (
        (n_kl, z.left_max, lefts, 0),
        (n_kr, z.right_max, rights, 1),
        (n_left, 0, lefts, 0),
        (n_right, 0, rights, 1),
    )

    if second:
        for count, start, place, which in kept:
            source = (lefts_in, rights_in)[which]

            @pl.loop(0, count)
            def _(k):
                pltpu.make_async_copy(
                    source.at[start + k], place.at[start + k], tile_sem
                ).start()

    else:

        def fetch(at_tile, low, slots, k):
            s = low + k % slots
            tile = plan[at_tile + k]
            array, at = tile // PLACES, tile % PLACES
            for which, source in enumerate(tiles):

                @pl.when(array == which)
                def _():
                    pltpu.make_async_copy(
                        source.at[at], ring.at[s], ring_sem.at[s]
                    ).start()

        queues = (
            (n_kl, z.at_kl_tile, 0, CAP),
            (n_kr, z.at_kr_tile, CAP, z.right_op),
            (n_left, z.at_left_tile, CAP + z.right_op, RING),
            (n_right, z.at_right_tile, CAP + z.right_op + RING, RING),
        )
        for count, at_tile, low, slots in queues:

            @pl.loop(0, jnp.minimum(count, slots))
            def _(k):
                fetch(at_tile, low, slots, k)

    n_read = plan[N_READ]

    @pl.loop(0, n_read)
    def _(k):
        block = plan[z.at_read + k]
        start_block(z, plan, base, changed, block, cur.at[block], cur_sem)

    hits = (N_HIT_OWN, z.at_hit_own) if second else (N_HIT_ALL, z.at_hit_all)
    load_blocks(z, plan, *hits, base, acc, acc_sem)

    if second:
        wait_each(
            n_tiles, pltpu.make_async_copy(lefts_in.at[0], lefts.at[0], tile_sem)
        )
    else:
        n_read = n_read + load_halo(z, plan, halo, cur, 0, cur_sem)

        def prepare(count, at_tile, low, slots, start, place, target, build):
            @pl.loop(0, count)
            def _(k):
                s = low + k % slots
                pltpu.make_async_copy(tiles[0].at[0], ring.at[s], ring_sem.at[s]).wait()
                quads = build(ring[s, 0], ring[s, 1])
                for part in (0, 1):
                    for row in (0, 1):
                        for col in (0, 1):
                            place[
                                start + k,
                                part,
                                row * edge : (row + 1) * edge,
                                col * edge : (col + 1) * edge,
                            ] = quads[row][col][part]
                pltpu.make_async_copy(
                    place.at[start + k], target.at[start + k], tile_sem
                ).start()

                @pl.when(k + slots < count)
                def _():
                    fetch(at_tile, low, slots, k + slots)

        def plain(re, im):
            minus = tuple(-part for part in im)
            return ((re, minus), (im, re))

        def turned(re, im):
            minus = tuple(-part for part in re)
            return ((im, re), (minus, im))

        def build_left(re, im):
            return plain(halves(re), halves(im))

        def build_right(re, im):
            return plain(halves((re * SCALE).T), halves((im * SCALE).T))

        def build_kr(re, im):
            return turned(halves((re * SCALE).T), halves((im * SCALE).T))

        def build_kl(re, im):
            return turned(halves(re * SCALE), halves(im * SCALE))

        prepare(*queues[0], z.left_max, lefts, lefts_out, build_kl)
        prepare(*queues[1], z.right_max, rights, rights_out, build_kr)
        prepare(*queues[2], 0, lefts, lefts_out, build_left)
        prepare(*queues[3], 0, rights, rights_out, build_right)

    wait_each(n_read, pltpu.make_async_copy(block_at(z, base, 0), cur.at[0], cur_sem))
    wait_each(
        plan[hits[0]], pltpu.make_async_copy(block_at(z, base, 0), acc.at[0], acc_sem)
    )
    work = Work(z, 2 if second else 1, plan, cur, acc, 0)

    def tile_of(store, slot):
        return store[slot, 0], store[slot, 1]

    @pl.loop(0, n_kl)
    def _(q):
        far = plan[z.at_kl_src + q] >= z.blocks

        @pl.when(jnp.logical_not(far) if second else True)
        def _():
            work.ham_left(q, tile_of(lefts, z.left_max + q))

    @pl.loop(0, n_kr)
    def _(q):
        far = plan[z.at_kr_src + q] >= z.blocks
        tile = tile_of(rights, z.right_max + q)

        @pl.when(jnp.logical_not(far))
        def _():
            work.ham_right(q, tile, False)

        if not second:

            @pl.when(far)
            def _():
                work.ham_right(q, tile, True)

    for count, side in ((N_OWN, "own"), (N_FAR, "far"))[: 1 if second else 2]:
        at_left = getattr(z, "at_" + side + "_left")
        at_right = getattr(z, "at_" + side + "_right")

        @pl.loop(0, groups(plan[count]))
        def _(g):
            work.pairs(
                side,
                g,
                lambda u, p: tile_of(lefts, plan[at_left + p]),
                lambda u, p: tile_of(rights, plan[at_right + p]),
            )

    store_blocks(z, plan, *hits, acc, out, out_sem)
    if not second:
        wait_each(
            n_tiles, pltpu.make_async_copy(lefts.at[0], lefts_out.at[0], tile_sem)
        )


def far_kernel(z, n_halo, plan, lefts_in, rights_in, result, *refs):
    halo = refs[:n_halo]
    out, cur, acc, lefts, rights, sems = refs[n_halo:]
    cur_sem, acc_sem, out_sem, tile_sem = (sems.at[k] for k in range(4))
    n_read = load_halo(z, plan, halo, cur, z.blocks, cur_sem)
    load_blocks(z, plan, N_HIT_FAR, z.at_hit_far, result, acc, acc_sem)
    wait_each(n_read, pltpu.make_async_copy(halo[2].at[0], cur.at[0], cur_sem))
    wait_each(
        plan[N_HIT_FAR],
        pltpu.make_async_copy(block_at(z, result, 0), acc.at[0], acc_sem),
    )
    work = Work(z, 2, plan, cur, acc, z.blocks)

    def bring(slot, source, place):
        copy = pltpu.make_async_copy(source.at[slot], place, tile_sem)
        copy.start()
        return copy

    @pl.loop(0, groups(plan[N_FAR]))
    def _(g):
        copies = []
        for u in range(UNROLL):
            p = g * UNROLL + u
            copies.append(bring(plan[z.at_far_left + p], lefts_in, lefts.at[u]))
            copies.append(bring(plan[z.at_far_right + p], rights_in, rights.at[u]))
        for copy in copies:
            copy.wait()
        work.pairs(
            "far",
            g,
            lambda u, p: (lefts[u, 0], lefts[u, 1]),
            lambda u, p: (rights[u, 0], rights[u, 1]),
        )

    @pl.loop(0, plan[N_KL])
    def _(q):
        @pl.when(plan[z.at_kl_src + q] >= z.blocks)
        def _():
            bring(z.left_max + q, lefts_in, lefts.at[0]).wait()
            work.ham_left(q, (lefts[0, 0], lefts[0, 1]))

    @pl.loop(0, plan[N_KR])
    def _(q):
        @pl.when(plan[z.at_kr_src + q] >= z.blocks)
        def _():
            bring(z.right_max + q, rights_in, rights.at[0]).wait()
            work.ham_right(q, (rights[0, 0], rights[0, 1]), True)

    store_blocks(z, plan, N_HIT_FAR, z.at_hit_far, acc, out, out_sem)


PARAMS = pltpu.CompilerParams(vmem_limit_bytes=58 * 1024 * 1024)


def copy_of(z, base):
    spec = pl.BlockSpec((2, z.edge, base.shape[2]), lambda r: (0, r, 0))

    def kernel(src, dst):
        dst[...] = src[...]

    return pl.pallas_call(
        kernel,
        out_shape=jax.ShapeDtypeStruct(base.shape, jnp.float32),
        grid=(z.rt,),
        in_specs=[spec],
        out_specs=spec,
        cost_estimate=pl.CostEstimate(
            flops=0, bytes_accessed=2 * base.size * 4, transcendentals=0
        ),
        name="copy_of",
    )(base)


def first_stage(z, plan, tiles, base, halo, result):
    block = (2, z.edge, z.edge)
    lefts = tile_shape(z, z.left_max + CAP)
    rights = tile_shape(z, z.right_max + z.right_op)
    return pl.pallas_call(
        functools.partial(stage_kernel, z, False),
        out_shape=[
            jax.ShapeDtypeStruct(base.shape, jnp.float32),
            jax.ShapeDtypeStruct(lefts, jnp.bfloat16),
            jax.ShapeDtypeStruct(rights, jnp.bfloat16),
        ],
        in_specs=[SMEM] + [ANY] * (2 + len(tiles) + len(halo)),
        out_specs=[ANY] * 3,
        scratch_shapes=[
            pltpu.VMEM((z.corner + 1,) + block, jnp.float32),
            pltpu.VMEM((z.blocks + 1,) + block, jnp.float32),
            pltpu.VMEM(lefts, jnp.bfloat16),
            pltpu.VMEM(rights, jnp.bfloat16),
            pltpu.VMEM((CAP + z.right_op + 2 * RING,) + block, jnp.float32),
            pltpu.SemaphoreType.DMA((CAP + z.right_op + 2 * RING,)),
            pltpu.SemaphoreType.DMA((3,)),
            pltpu.SemaphoreType.DMA,
        ],
        compiler_params=PARAMS,
        cost_estimate=COST,
        name="stage_one",
    )(plan, *tiles, base, *halo, result)


COST = pl.CostEstimate(flops=4_000_000_000, bytes_accessed=48_000_000, transcendentals=0)


def second_stage(z, plan, lefts, rights, base, middle, result):
    block = (2, z.edge, z.edge)
    return pl.pallas_call(
        functools.partial(stage_kernel, z, True),
        out_shape=jax.ShapeDtypeStruct(base.shape, jnp.float32),
        in_specs=[SMEM] + [ANY] * 5,
        out_specs=ANY,
        scratch_shapes=[
            pltpu.VMEM((z.blocks,) + block, jnp.float32),
            pltpu.VMEM((z.blocks + 1,) + block, jnp.float32),
            pltpu.VMEM(lefts.shape, jnp.bfloat16),
            pltpu.VMEM(rights.shape, jnp.bfloat16),
            pltpu.VMEM((1,) + block, jnp.float32),
            pltpu.SemaphoreType.DMA((1,)),
            pltpu.SemaphoreType.DMA((3,)),
            pltpu.SemaphoreType.DMA,
        ],
        input_output_aliases={5: 0},
        compiler_params=PARAMS,
        cost_estimate=COST,
        name="stage_two",
    )(plan, lefts, rights, base, middle, result)


def far_stage(z, plan, lefts, rights, result, halo):
    block = (2, z.edge, z.edge)
    return pl.pallas_call(
        functools.partial(far_kernel, z, len(halo)),
        out_shape=jax.ShapeDtypeStruct(result.shape, jnp.float32),
        in_specs=[SMEM] + [ANY] * (3 + len(halo)),
        out_specs=ANY,
        scratch_shapes=[
            pltpu.VMEM((z.corner + 1 - z.blocks,) + block, jnp.float32),
            pltpu.VMEM((z.blocks + 1,) + block, jnp.float32),
            pltpu.VMEM(tile_shape(z, UNROLL), jnp.bfloat16),
            pltpu.VMEM(tile_shape(z, UNROLL), jnp.bfloat16),
            pltpu.SemaphoreType.DMA((4,)),
        ],
        input_output_aliases={3: 0},
        compiler_params=PARAMS,
        name="far",
    )(plan, lefts, rights, result, *halo)


def swapped(value, row_mask, col_mask):
    n, m = lax.axis_size("row"), lax.axis_size("col")
    if not col_mask:
        return lax.ppermute(value, "row", [(i, i ^ row_mask) for i in range(n)])
    if not row_mask:
        return lax.ppermute(value, "col", [(j, j ^ col_mask) for j in range(m)])
    route = [
        (i * m + j, (i ^ row_mask) * m + (j ^ col_mask)) for i in range(n) for j in range(m)
    ]
    return lax.ppermute(value, BOTH, route)


def near_tiles(own):
    return [swapped(own, *mask) for mask in ((4, 0), (2, 0), (0, 2), (1, 0), (1, 2))]


def gather_tiles(own, near, settle):
    z4, z2, x, y, d = near
    line = jnp.concatenate([z2, z4], axis=0)
    first = jnp.concatenate([own, line, x, y, d], axis=0)
    z6 = swapped(z4, 2, 0)
    x_line = swapped(line, 0, 2)
    y_line = swapped(line, 1, 0)
    d4 = swapped(d, 4, 0)
    d2 = swapped(d, 2, 0)
    (z6, x_line, y_line, d4, d2, first), kept = settle((z6, x_line, y_line, d4, d2, first))
    last = [swapped(z6, 0, 2), swapped(z6, 1, 0), swapped(d4, 2, 0)]
    first_other = swapped(first, 0, 1)
    second = jnp.concatenate([z6, x_line, y_line, d4, d2], axis=0)
    second_other = swapped(second, 0, 1)
    third = jnp.concatenate(last, axis=0)
    third_other = swapped(third, 0, 1)
    return [first, second, third, first_other, second_other, third_other], kept


HOPS = (
    (0, 0), (0, 4), (0, 3), (0, 5),
    (0, 1), (1, 3), (1, 1), (1, 6),
    (0, 2), (1, 4), (1, 2), (1, 5),
    (1, 0), (2, 1), (2, 0), (2, 2),
)


def local(state, tile_vals, tile_row, tile_col, tile_op):
    z = Sizes(state, tile_vals)
    meta = jnp.stack([tile_row, tile_col, tile_op])
    spread = jnp.broadcast_to(meta[None], (z.row_total * z.col_total,) + meta.shape)
    gathered = lax.all_to_all(spread, BOTH, 0, 0, tiled=True)
    if z.by_hops:
        near = near_tiles(tile_vals)
    else:
        tiles = [lax.all_gather(tile_vals, BOTH, axis=0, tiled=True)]
    meta = jnp.swapaxes(gathered, 0, 1).reshape(3, z.total)
    table = [jnp.int32(array * PLACES + at) for array, at in HOPS]
    here = jnp.stack(
        [lax.axis_index("row").astype(jnp.int32), lax.axis_index("col").astype(jnp.int32)]
        + table
    )
    plan = make_plan(z, here, meta.reshape(-1))
    kind = extra_kind(z, meta[0], meta[1], meta[2])
    packed = pack(z, plan, state, None, True, z.row_slots, z.col_slots)
    if z.by_hops:
        near, plan, packed = lax.optimization_barrier((near, plan, packed))
    halo = exchange(z, plan, kind, state, None, packed)
    result = copy_of(z, state)
    if z.by_hops:

        def settle(values):
            return lax.optimization_barrier((values, (halo, result)))

        tiles, (halo, result) = gather_tiles(tile_vals, near, settle)
    middle, lefts, rights = first_stage(z, plan, tiles, state, halo, result)
    packed = pack(z, plan, state, middle, True, z.row_slots, z.col_slots)
    halo = exchange(z, plan, kind, state, middle, packed)
    result = second_stage(z, plan, lefts, rights, state, middle, result)
    return far_stage(z, plan, lefts, rights, result, halo)


def solution(mesh):
    placed = (
        P(None, "row", "col"),
        P(("row", "col"), None, None, None),
        P(("row", "col")),
        P(("row", "col")),
        P(("row", "col")),
    )
    return jax.shard_map(
        local, mesh=mesh, in_specs=placed, out_specs=P(None, "row", "col"), check_vma=False
    )
```
